512 devices in a mesh: clus: 64 (over x, z_hi, y), samp: 8 (over z_lo, core).
Axes of the slice: x: 4, y: 4, z: 16 (z_hi: 4, z_lo: 4; z = z_hi * 4 + z_lo), core: 2. Of those that a mesh axis runs over, the one named last changes fastest.
Arguments:
- child_patterns: float32 [2048, 2, 24, 512], P('clus', None, 'samp'), may hold values from -6 to 6
- theta_weights: float32 [6, 9], replicated, may hold values from -0.4 to 0.6
- phi_stencil: int32 [1024, 6], replicated, may hold values from 0 to 511, as said below
- phi_weights: float32 [1024, 6], replicated, may hold values from -0.3 to 0.7
- shift_phase: float32 [8, 48, 1024], P(None, 'samp'), may hold values from -3.140625 to 3.140625
- translation_table: float32 [16, 2, 48, 1024], P(None, None, 'samp', 'clus'), may hold values from -1.25 to 1.25
- far_list: int32 [256, 12], replicated, may hold values from 0 to 255, as said below
- far_vector: int32 [256, 12], replicated, may hold values from 0 to 15
Outputs:
- parent_incoming: float32 [256, 2, 48, 1024], P('clus', None, 'samp')
- child_incoming: float32 [2048, 2, 24, 512], P('clus', None, 'samp')
The draws below stay inside these ranges and needn't reach their ends.
Inputs may be any that keep to these rules, and one draw needn't show every extreme that they name: `far_list`: row i names 12 different parent clusters, never i itself. `phi_stencil`: row n names 6 cyclically consecutive child columns starting at n // 2 - 6 // 2 + 1 or one column later.
All inputs are finite; a program needn't handle non-finite values.
Results may differ from the reference program's by a relative error of at most 0.00007.
Values sent between devices are 32-bit elements; how exact they have to be, the bound alone decides.
A program may use at most 128 MiB of HBM per device.

```python
import jax
import jax.numpy as jnp
from jax import lax

TR_DEV = 6
NPH = 1024
NPC = 512
P_SIZE = 6
L = 12
NV = 16
NCL = 256
NCH = 2048
TR = 48
TRC = 24


def draw_far_list(key, part):
    keys = jax.random.split(jax.random.fold_in(key, 11), NCL)

    def single(row_key):
        return jax.random.permutation(row_key, NCL - 1)[:L]
    offsets = jax.vmap(single)(keys).astype(jnp.int32)
    owners = jnp.arange(NCL, dtype=jnp.int32)[:, None]
    return ((owners + 1 + offsets) % NCL).astype(jnp.int32)


def draw_phi_stencil(key, part):
    columns = jnp.arange(NPH, dtype=jnp.int32)
    extra = jax.random.randint(jax.random.fold_in(key, 23), (NPH,), 0, 2).astype(jnp.int32)
    start = columns // 2 - P_SIZE // 2 + 1 + extra
    points = jnp.arange(P_SIZE, dtype=jnp.int32)
    return ((start[:, None] + points[None, :]) % NPC).astype(jnp.int32)


def set_ends(result, own_key, smallest, high):
    dims = result.shape
    place = [jax.random.randint(jax.random.fold_in(own_key, axis), (), 0, dims[axis]) for axis in range(len(dims))]
    result = result.at[tuple(place)].set(smallest)
    longest = dims.index(max(dims))
    place[longest] = (place[longest] + 1) % dims[longest]
    return result.at[tuple(place)].set(high)


def levels(rng, extent, cuts, smallest, top_value):
    loudness, own = 1.0, jax.random.fold_in(rng, 6)
    for position, shards_of in cuts:
        heights = jnp.exp(jax.random.uniform(jax.random.fold_in(own, position), (shards_of,), jnp.float32, smallest / len(cuts), top_value / len(cuts)))
        loudness = loudness * jnp.repeat(heights, extent[position] // shards_of).reshape([-1 if axis == position else 1 for axis in range(len(extent))])
    return loudness


def normal_values(rng, extent, scale, limit, shards=(), kind=jnp.bfloat16):
    gain = levels(rng, extent, shards, -0.22, 0.18) if shards else 1.0
    result = jax.random.normal(rng, extent, jnp.float32) * scale * gain
    return jnp.minimum(jnp.maximum(result, -limit), limit).astype(kind)


def setup_inputs(seed: int = 0) -> dict:
    splits = jax.random.split(jax.random.key(seed), 9)
    return {
        "child_patterns": normal_values(splits[0], (NCH, 2, TRC, NPC), 1.0, 6.0, ((0, 64), (2, 8)), jnp.float32),
        "theta_weights": jnp.clip(jax.random.uniform(splits[1], (TR_DEV, TR_DEV // 2 + P_SIZE), jnp.float32, -0.4, 0.6), -0.4, 0.6),
        "phi_stencil": draw_phi_stencil(jax.random.fold_in(splits[8], 71), 0),
        "phi_weights": jnp.clip(jax.random.uniform(splits[3], (NPH, P_SIZE), jnp.float32, -0.3, 0.7), -0.3, 0.7),
        "shift_phase": jnp.clip(jax.random.uniform(splits[4], (8, TR, NPH), jnp.float32, -3.140625, 3.140625), -3.140625, 3.140625),
        "translation_table": normal_values(splits[5], (NV, 2, TR, NPH), (2 * L) ** -0.5, 1.25, ((2, 8), (3, 64)), jnp.float32),
        "far_list": draw_far_list(jax.random.fold_in(splits[8], 71), 0),
        "far_vector": set_ends(jax.random.randint(splits[7], (NCL, L), 0, NV), jax.random.fold_in(splits[7], 1), 0, NV - 1).astype(jnp.int32),
    }


def phi_table(phi_stencil, phi_weights):
    positions = jnp.arange(NPC, dtype=jnp.int32)
    total = jnp.zeros((NPC, NPH), jnp.float32)
    for point in range(P_SIZE):
        hits = (phi_stencil[None, :, point] == positions[:, None]).astype(jnp.float32)
        total = total + hits * phi_weights[None, :, point]
    return total


def theta_table(theta_weights):
    rows = jnp.arange(TR, dtype=jnp.int32)
    owner = rows // TR_DEV
    local = rows % TR_DEV
    child_rows = jnp.arange(TRC, dtype=jnp.int32)
    total = jnp.zeros((TR, TRC), jnp.float32)
    for point in range(TR_DEV // 2 + P_SIZE):
        target = (owner * (TR_DEV // 2) - P_SIZE // 2 + point) % TRC
        hits = (target[:, None] == child_rows[None, :]).astype(jnp.float32)
        total = total + hits * theta_weights[local, point][:, None]
    return total


def reference(child_patterns, theta_weights, phi_stencil, phi_weights, shift_phase, translation_table, far_list, far_vector):
    highest = lax.Precision.HIGHEST
    phi_matrix = phi_table(phi_stencil, phi_weights)
    theta_matrix = theta_table(theta_weights)
    cosine = jnp.cos(shift_phase)
    sine = jnp.sin(shift_phase)

    def aggregate(family):
        spread = jnp.einsum("cqtp,pn->cqtn", family, phi_matrix, precision=highest)
        refined = jnp.einsum("rt,cqtn->cqrn", theta_matrix, spread, precision=highest)
        real_part = refined[:, 0] * cosine - refined[:, 1] * sine
        imag_part = refined[:, 0] * sine + refined[:, 1] * cosine
        return jnp.stack([jnp.sum(real_part, axis=0), jnp.sum(imag_part, axis=0)], axis=0)

    outgoing = lax.map(aggregate, child_patterns.reshape(NCL, 8, 2, TRC, NPC))

    def translate(entry):
        far_ids, vec_ids = entry
        source = outgoing[far_ids]
        operator = translation_table[vec_ids]
        real_part = operator[:, 0] * source[:, 0] - operator[:, 1] * source[:, 1]
        imag_part = operator[:, 0] * source[:, 1] + operator[:, 1] * source[:, 0]
        return jnp.stack([jnp.sum(real_part, axis=0), jnp.sum(imag_part, axis=0)], axis=0)

    parent_incoming = lax.map(translate, (far_list, far_vector))

    def disaggregate(field):
        low_real = field[None, 0] * cosine + field[None, 1] * sine
        low_imag = field[None, 1] * cosine - field[None, 0] * sine
        lowered = jnp.stack([low_real, low_imag], axis=1)
        coarse = jnp.einsum("rt,cqrn->cqtn", theta_matrix, lowered, precision=highest)
        return jnp.einsum("cqtn,pn->cqtp", coarse, phi_matrix, precision=highest)

    child_incoming = lax.map(disaggregate, parent_incoming).reshape(NCH, 2, TRC, NPC)
    return parent_incoming, child_incoming
```

```python
import jax
import jax.numpy as jnp
from jax import lax
from jax.sharding import PartitionSpec as P

P_SIZE = 6
HIGH = lax.Precision.HIGH


def shifted(value, axis, by):
    peers = lax.axis_size(axis)
    return lax.ppermute(value, axis, [(i, (i + by) % peers) for i in range(peers)])


def phi_table(phi_stencil, phi_weights, columns):
    positions = jnp.arange(columns, dtype=jnp.int32)
    total = jnp.zeros((columns, phi_stencil.shape[0]), jnp.float32)
    for point in range(phi_stencil.shape[1]):
        hits = (phi_stencil[None, :, point] == positions[:, None]).astype(jnp.float32)
        total = total + hits * phi_weights[None, :, point]
    return total


def per_device(
    child_patterns,
    theta_weights,
    phi_stencil,
    phi_weights,
    shift_phase,
    translation_table,
    far_list,
    far_vector,
):
    groups = child_patterns.shape[0] // 8
    columns = child_patterns.shape[3]
    rows_parent = theta_weights.shape[0]
    azimuth = phi_stencil.shape[0]
    margin = P_SIZE // 2
    below = shifted(child_patterns, "samp", 1)
    above = shifted(child_patterns, "samp", -1)
    phi_matrix = phi_table(phi_stencil, phi_weights, columns)
    cosine = jnp.cos(shift_phase)
    sine = jnp.sin(shift_phase)
    extended = jnp.concatenate([below, child_patterns, above], axis=2)
    tilted = jnp.stack(
        [sum(theta_weights[a, b] * extended[:, :, b] for b in range(9)) for a in range(rows_parent)],
        axis=2,
    )
    refined = jnp.einsum("cqap,pn->cqan", tilted, phi_matrix, precision=HIGH)
    refined = refined.reshape(groups, 8, 2, rows_parent, azimuth)
    real_part = refined[:, :, 0] * cosine - refined[:, :, 1] * sine
    imag_part = refined[:, :, 0] * sine + refined[:, :, 1] * cosine
    outgoing = jnp.stack([jnp.sum(real_part, axis=1), jnp.sum(imag_part, axis=1)], axis=1)
    everyone = lax.all_to_all(outgoing, "clus", split_axis=3, concat_axis=0, tiled=True)
    clusters = everyone.shape[0]
    lanes = everyone.shape[2] * everyone.shape[3]
    flat = everyone.reshape(clusters, 2 * lanes)
    table = translation_table.reshape(translation_table.shape[0], 2 * lanes)
    pick = (far_list[:, :, None] == jnp.arange(clusters)[None, None, :]).astype(jnp.float32)
    pick_vec = (far_vector[:, :, None] == jnp.arange(table.shape[0])[None, None, :]).astype(jnp.float32)
    source = jnp.einsum("ilc,cs->lis", pick, flat, precision=HIGH)
    operator = jnp.einsum("ilv,vs->lis", pick_vec, table, precision=HIGH)
    s_re, s_im = source[..., :lanes], source[..., lanes:]
    o_re, o_im = operator[..., :lanes], operator[..., lanes:]
    in_re = jnp.sum(o_re * s_re - o_im * s_im, axis=0)
    in_im = jnp.sum(o_re * s_im + o_im * s_re, axis=0)
    landed = jnp.concatenate([in_re, in_im], axis=1).reshape(everyone.shape)
    incoming = lax.all_to_all(landed, "clus", split_axis=0, concat_axis=3, tiled=True)
    low_real = incoming[:, None, 0] * cosine + incoming[:, None, 1] * sine
    low_imag = incoming[:, None, 1] * cosine - incoming[:, None, 0] * sine
    lowered = jnp.stack([low_real, low_imag], axis=2).reshape(groups * 8, 2, rows_parent, azimuth)
    narrow = jnp.einsum("cqan,pn->cqap", lowered, phi_matrix, precision=HIGH)

    def back(first):
        return jnp.stack(
            [sum(theta_weights[a, b] * narrow[:, :, a] for a in range(rows_parent)) for b in range(first, first + margin)],
            axis=2,
        )

    from_above = shifted(back(0), "samp", -1)
    from_below = shifted(back(2 * margin), "samp", 1)
    child_incoming = back(margin) + from_above + from_below
    return (incoming, child_incoming)


def solution(mesh):
    placed = (
        P("clus", None, "samp", None),
        P(),
        P(),
        P(),
        P(None, "samp", None),
        P(None, None, "samp", "clus"),
        P(),
        P(),
    )
    return jax.shard_map(
        per_device,
        mesh=mesh,
        in_specs=placed,
        out_specs=(P("clus", None, "samp", None), P("clus", None, "samp", None)),
        check_vma=False,
    )
```

```python
import functools

import jax
import jax.numpy as jnp
from jax import lax
from jax.experimental import pallas as pl
from jax.experimental.pallas import tpu as pltpu
from jax.sharding import PartitionSpec as P

MESH = pl.DeviceIdType.MESH
F32 = jnp.float32
BF16 = jnp.bfloat16


def halves(value):
    high = value.astype(BF16)
    return high, (value - high.astype(F32)).astype(BF16)


def dot(a, b, contract):
    return lax.dot_general(a, b, ((contract[0], contract[1]), ((), ())), preferred_element_type=F32)


def dot3(a_hi, a_lo, b_hi, b_lo, contract):
    return dot(a_hi, b_hi, contract) + (dot(a_hi, b_lo, contract) + dot(a_lo, b_hi, contract))


def window(
    n_clus, n_samp,
    theta, child, stencil, weights, phase, table, far, vec,
    inc_out, child_out,
    phi_hi, phi_lo, cosine, sine, picks, operators,
    below, above, lhs_hi, lhs_lo, low_hi, low_lo,
    msg_out, msg_in, back_out, back_in, rim_low, rim_high, got_above, got_below,
    halo_send, halo_recv, a2a_send, a2a_recv, own_sem, back_send, back_recv, rim_send, rim_recv,
):
    me = lax.axis_index("clus")
    ring = lax.axis_index("samp")
    up = lax.rem(ring + 1, n_samp)
    down = lax.rem(ring + n_samp - 1, n_samp)
    columns = child.shape[2]
    azimuth = stencil.shape[1]
    rows = phase.shape[1]
    far_count = far.shape[1]
    blocks = azimuth // 128
    per_block = n_clus // blocks
    width = 128 // per_block

    barrier = pltpu.get_barrier_semaphore()
    for side in (up, down):
        pl.semaphore_signal(barrier, inc=1, device_id=(me, side), device_id_type=MESH)

    def greet(step, carry):
        pl.semaphore_signal(barrier, inc=1, device_id=(lax.rem(me + step, n_clus), ring), device_id_type=MESH)
        return carry

    lax.fori_loop(1, n_clus, greet, 0)

    def build(step, carry):
        first = pl.multiple_of(step * 32, 32)
        places = lax.broadcasted_iota(jnp.int32, (32, azimuth), 0) + first
        total = jnp.zeros((32, azimuth), F32)
        for point in range(stencil.shape[0]):
            total = total + jnp.where(stencil[point : point + 1, :] == places, weights[point : point + 1, :], 0.0)
        high, low = halves(total)
        phi_hi[pl.ds(first, 32), :] = high
        phi_lo[pl.ds(first, 32), :] = low
        return carry

    lax.fori_loop(0, columns // 32, build, 0)

    pl.semaphore_wait(barrier, n_clus + 1)
    halos = [
        pltpu.make_async_remote_copy(
            src_ref=child, dst_ref=below, send_sem=halo_send.at[0], recv_sem=halo_recv.at[0],
            device_id=(me, up), device_id_type=MESH,
        ),
        pltpu.make_async_remote_copy(
            src_ref=child, dst_ref=above, send_sem=halo_send.at[1], recv_sem=halo_recv.at[1],
            device_id=(me, down), device_id_type=MESH,
        ),
    ]
    for copy in halos:
        copy.start()

    for octant in range(8):
        angle = phase[octant]
        cosine[octant] = jnp.cos(angle)
        sine[octant] = jnp.sin(angle)

    clusters = far.shape[0]
    t_hi, t_lo = halves(table[...])
    places = lax.broadcasted_iota(jnp.int32, (clusters, clusters), 1)
    kinds = lax.broadcasted_iota(jnp.int32, (clusters, table.shape[0]), 1)
    for link in range(far_count):
        picks[link] = jnp.where(far[:, link : link + 1] == places, 1.0, 0.0).astype(BF16)
        chosen = jnp.where(vec[:, link : link + 1] == kinds, 1.0, 0.0).astype(BF16)
        operators[link] = dot(chosen, t_hi, ((1,), (0,))) + dot(chosen, t_lo, ((1,), (0,)))

    for copy in halos:
        copy.wait()

    for row in range(rows):
        total = jnp.zeros((64, columns), F32)
        for step in range(9):
            part = (below, child, above)[step // 3][step % 3]
            total = total + theta[row, step] * part
        high, low = halves(total)
        lhs_hi[row * 64 : (row + 1) * 64, :] = high
        lhs_lo[row * 64 : (row + 1) * 64, :] = low

    half = lax.broadcasted_iota(jnp.int32, (8, 128), 0) < 4
    group = lax.broadcasted_iota(jnp.int32, (8, 128), 1) // width

    for block in range(blocks):
        lanes = slice(block * 128, (block + 1) * 128)
        refined = dot3(lhs_hi[...], lhs_lo[...], phi_hi[:, lanes], phi_lo[:, lanes], ((1,), (0,)))
        fields = []
        for row in range(rows):
            straight = jnp.zeros((8, 128), F32)
            crossed = jnp.zeros((8, 128), F32)
            for octant in range(8):
                piece = refined[row * 64 + octant * 8 : row * 64 + octant * 8 + 8]
                straight = straight + piece * cosine[octant, row : row + 1, lanes]
                crossed = crossed + piece * sine[octant, row : row + 1, lanes]
            crossed = pltpu.roll(crossed, 4, 0)
            fields.append(straight + jnp.where(half, -crossed, crossed))
        for part in range(per_block):
            packed = jnp.zeros((8, 128), F32)
            for row in range(rows):
                moved = pltpu.roll(fields[row], ((row - part) * width) % 128, 1)
                packed = jnp.where(group == row, moved, packed)
            msg_out[block * per_block + part] = packed
        for part in range(per_block):
            target = block * per_block + part

            @pl.when(target != me)
            def _():
                pltpu.make_async_remote_copy(
                    src_ref=msg_out.at[target], dst_ref=msg_in.at[me], send_sem=a2a_send, recv_sem=a2a_recv,
                    device_id=(target, ring), device_id_type=MESH,
                ).start()

    own = pltpu.make_async_copy(msg_out.at[me], msg_in.at[me], own_sem.at[0])
    own.start()
    own.wait()
    others = pl.ds(0, n_clus - 1)
    pltpu.make_async_copy(msg_out.at[others], msg_in.at[others], a2a_recv).wait()

    pairs = n_clus // 2
    arrived = msg_in[...].reshape(pairs, 2, 8, 128)
    even, odd = arrived[:, 0], arrived[:, 1]
    half_b = lax.broadcasted_iota(jnp.int32, (pairs, 8, 128), 1) < 4
    real = jnp.where(half_b, even, pltpu.roll(odd, 4, 1)).reshape(clusters, 128)
    imag = jnp.where(half_b, pltpu.roll(even, 4, 1), odd).reshape(clusters, 128)
    x_hi, x_lo = halves(jnp.concatenate([real, imag], axis=1))
    in_re = jnp.zeros((clusters, 128), F32)
    in_im = jnp.zeros((clusters, 128), F32)
    for link in range(far_count):
        pick = picks[link]
        source = dot(pick, x_hi, ((1,), (0,))) + dot(pick, x_lo, ((1,), (0,)))
        s_re, s_im = source[:, :128], source[:, 128:]
        o_re, o_im = operators[link, :, :128], operators[link, :, 128:]
        in_re = in_re + (o_re * s_re - o_im * s_im)
        in_im = in_im + (o_re * s_im + o_im * s_re)
    in_re = in_re.reshape(pairs, 8, 128)
    in_im = in_im.reshape(pairs, 8, 128)
    back_even = jnp.where(half_b, in_re, pltpu.roll(in_im, 4, 1))
    back_odd = jnp.where(half_b, pltpu.roll(in_re, 4, 1), in_im)
    back_out[...] = jnp.stack([back_even, back_odd], axis=1).reshape(n_clus, 8, 128)

    def give(step, carry):
        target = lax.rem(me + step, n_clus)
        pltpu.make_async_remote_copy(
            src_ref=back_out.at[target], dst_ref=back_in.at[me], send_sem=back_send, recv_sem=back_recv,
            device_id=(target, ring), device_id_type=MESH,
        ).start()
        return carry

    lax.fori_loop(1, n_clus, give, 0)
    own = pltpu.make_async_copy(back_out.at[me], back_in.at[me], own_sem.at[1])
    own.start()
    own.wait()
    pltpu.make_async_copy(back_out.at[others], back_in.at[others], back_recv).wait()

    for block in range(blocks):
        lanes = slice(block * 128, (block + 1) * 128)
        for row in range(rows):
            field = jnp.zeros((8, 128), F32)
            for part in range(per_block):
                moved = pltpu.roll(back_in[block * per_block + part], ((part - row) * width) % 128, 1)
                field = jnp.where(group == part, moved, field)
            inc_out[row, :, lanes] = field
            swapped = pltpu.roll(field, 4, 0)
            swapped = jnp.where(half, swapped, -swapped)
            for octant in range(0, 8, 2):
                pieces = [
                    field * cosine[o, row : row + 1, lanes] + swapped * sine[o, row : row + 1, lanes]
                    for o in (octant, octant + 1)
                ]
                high, low = halves(jnp.concatenate(pieces, axis=0))
                low_hi[row * 64 + octant * 8 : row * 64 + octant * 8 + 16, lanes] = high
                low_lo[row * 64 + octant * 8 : row * 64 + octant * 8 + 16, lanes] = low

    for cut in range(0, columns, 256):
        span = slice(cut, cut + 256)
        narrow = dot3(low_hi[...], low_lo[...], phi_hi[span, :], phi_lo[span, :], ((1,), (1,)))
        for step in range(9):
            total = jnp.zeros((64, 256), F32)
            for row in range(rows):
                total = total + theta[row, step] * narrow[row * 64 : (row + 1) * 64]
            (rim_low, child_out, rim_high)[step // 3][step % 3, :, span] = total

    rims = [
        pltpu.make_async_remote_copy(
            src_ref=rim_low, dst_ref=got_above, send_sem=rim_send.at[0], recv_sem=rim_recv.at[0],
            device_id=(me, down), device_id_type=MESH,
        ),
        pltpu.make_async_remote_copy(
            src_ref=rim_high, dst_ref=got_below, send_sem=rim_send.at[1], recv_sem=rim_recv.at[1],
            device_id=(me, up), device_id_type=MESH,
        ),
    ]
    for copy in rims:
        copy.start()
    pltpu.make_async_copy(msg_out.at[others], msg_in.at[others], a2a_send).wait()
    pltpu.make_async_copy(back_out.at[others], back_in.at[others], back_send).wait()
    for copy in rims:
        copy.wait()
    child_out[...] = child_out[...] + got_above[...] + got_below[...]


def per_device(n_clus, n_samp, child_patterns, theta_weights, phi_stencil, phi_weights, shift_phase, translation_table, far_list, far_vector):
    groups = child_patterns.shape[0] // 8
    own_rows, columns = child_patterns.shape[2:]
    rows = theta_weights.shape[0]
    azimuth = phi_stencil.shape[0]
    clusters, far_count = far_list.shape
    kinds = translation_table.shape[0]
    child = child_patterns.reshape(groups, 8, 2, own_rows, columns).transpose(3, 1, 2, 0, 4)
    child = child.reshape(own_rows, groups * 16, columns)
    lanes = rows * translation_table.shape[3]
    table = jnp.pad(translation_table.reshape(kinds, 2, lanes), ((0, 0), (0, 0), (0, 128 - lanes)))
    table = table.reshape(kinds, 256)
    vmem = pl.BlockSpec(memory_space=pltpu.VMEM)
    smem = pl.BlockSpec(memory_space=pltpu.SMEM)
    block = (own_rows, groups * 16, columns)
    incoming, child_incoming = pl.pallas_call(
        functools.partial(window, n_clus, n_samp),
        out_shape=(
            jax.ShapeDtypeStruct((rows, 8, azimuth), F32),
            jax.ShapeDtypeStruct(block, F32),
        ),
        in_specs=[smem] + [vmem] * 7,
        out_specs=(vmem, vmem),
        scratch_shapes=[
            pltpu.VMEM((columns, azimuth), BF16),
            pltpu.VMEM((columns, azimuth), BF16),
            pltpu.VMEM((8, rows, azimuth), F32),
            pltpu.VMEM((8, rows, azimuth), F32),
            pltpu.VMEM((far_count, clusters, clusters), BF16),
            pltpu.VMEM((far_count, clusters, 256), F32),
            pltpu.VMEM(block, F32),
            pltpu.VMEM(block, F32),
            pltpu.VMEM((rows * 64, columns), BF16),
            pltpu.VMEM((rows * 64, columns), BF16),
            pltpu.VMEM((rows * 64, azimuth), BF16),
            pltpu.VMEM((rows * 64, azimuth), BF16),
            pltpu.VMEM((n_clus, 8, 128), F32),
            pltpu.VMEM((n_clus, 8, 128), F32),
            pltpu.VMEM((n_clus, 8, 128), F32),
            pltpu.VMEM((n_clus, 8, 128), F32),
            pltpu.VMEM(block, F32),
            pltpu.VMEM(block, F32),
            pltpu.VMEM(block, F32),
            pltpu.VMEM(block, F32),
            pltpu.SemaphoreType.DMA((2,)),
            pltpu.SemaphoreType.DMA((2,)),
            pltpu.SemaphoreType.DMA,
            pltpu.SemaphoreType.DMA,
            pltpu.SemaphoreType.DMA((2,)),
            pltpu.SemaphoreType.DMA,
            pltpu.SemaphoreType.DMA,
            pltpu.SemaphoreType.DMA((2,)),
            pltpu.SemaphoreType.DMA((2,)),
        ],
        compiler_params=pltpu.CompilerParams(collective_id=0, has_side_effects=True, vmem_limit_bytes=48 << 20),
    )(theta_weights, child, phi_stencil.T, phi_weights.T, shift_phase, table, far_list, far_vector)
    incoming = incoming.reshape(rows, 2, groups, azimuth).transpose(2, 1, 0, 3)
    child_incoming = child_incoming.reshape(own_rows, 8, 2, groups, columns).transpose(3, 1, 2, 0, 4)
    return incoming, child_incoming.reshape(child_patterns.shape)


def solution(mesh):
    placed = (
        P("clus", None, "samp", None),
        P(),
        P(),
        P(),
        P(None, "samp", None),
        P(None, None, "samp", "clus"),
        P(),
        P(),
    )
    return jax.shard_map(
        functools.partial(per_device, mesh.shape["clus"], mesh.shape["samp"]),
        mesh=mesh,
        in_specs=placed,
        out_specs=(P("clus", None, "samp", None), P("clus", None, "samp", None)),
        check_vma=False,
    )
```

```python
import functools

import jax
import jax.numpy as jnp
from jax import lax
from jax.experimental import pallas as pl
from jax.experimental.pallas import tpu as pltpu
from jax.sharding import PartitionSpec as P

MESH = pl.DeviceIdType.MESH
F32 = jnp.float32
BF16 = jnp.bfloat16


def halves(value):
    high = value.astype(BF16)
    return high, (value - high.astype(F32)).astype(BF16)


def dot(a, b, contract):
    return lax.dot_general(a, b, ((contract[0], contract[1]), ((), ())), preferred_element_type=F32)


def dot3(a_hi, a_lo, b_hi, b_lo, contract):
    return dot(a_hi, b_hi, contract) + (dot(a_hi, b_lo, contract) + dot(a_lo, b_hi, contract))


def swap_groups(value):
    row = lax.broadcasted_iota(jnp.int32, (8, 128), 0)
    group = lax.broadcasted_iota(jnp.int32, (8, 128), 1) // 16
    for bit in (4, 2, 1):
        own, other = (row // bit) % 2, (group // bit) % 2
        rise = pltpu.roll(pltpu.roll(value, 8 - bit, 1), 16 * bit, 2)
        fall = rise if bit == 4 else pltpu.roll(pltpu.roll(value, bit, 1), 128 - 16 * bit, 2)
        value = jnp.where((own == other)[None], value, jnp.where((own < other)[None], rise, fall))
    return value


def window(
    n_clus, n_samp,
    theta, child, stencil_in, weights_in, phase_in, table_in, far_in, vec_in,
    inc_out, child_out,
    stencil, weights, phase, table, far, vec,
    phi_hi, phi_lo, cosine, sine, picks, operators,
    below, above, lhs_hi, lhs_lo, low_hi, low_lo, total_low,
    msg_out, msg_in, back_out, back_in, inc_pair, inc_far,
    in_sem, halo_send, halo_recv, phase_send, phase_recv,
    a2a_send, a2a_recv, own_sem, back_send, back_recv, inc_send, inc_recv,
):
    me = lax.axis_index("clus")
    ring = lax.axis_index("samp")
    up = lax.rem(ring + 1, n_samp)
    down = lax.rem(ring + n_samp - 1, n_samp)
    core = lax.rem(ring, 2)
    pair = ring + 1 - 2 * core
    away = lax.rem(ring + n_samp - 1 + 2 * core, n_samp)
    deep = lax.rem(lax.div(me, 4), 4)
    first_end = jnp.where(ring == 0, 3, 0)
    last_end = jnp.where(ring == n_samp - 1, 1, 0)
    near = me + 4 * (lax.rem(deep + first_end + last_end, 4) - deep)
    columns = child.shape[2]
    azimuth = stencil.shape[1]
    rows = phase.shape[0]
    far_count, clusters = far.shape
    others = pl.ds(0, n_clus - 1)

    loads = [
        pltpu.make_async_copy(source, target, in_sem.at[place])
        for place, (source, target) in enumerate(
            [(stencil_in, stencil), (weights_in, weights), (phase_in, phase), (table_in, table), (far_in, far), (vec_in, vec)]
        )
    ]
    for copy in loads:
        copy.start()

    barrier = pltpu.get_barrier_semaphore()
    for peer in ((me, up), (me, down), (near, away)):
        pl.semaphore_signal(barrier, inc=1, device_id=peer, device_id_type=MESH)

    def greet(step, carry):
        pl.semaphore_signal(barrier, inc=1, device_id=(lax.rem(me + step, n_clus), ring), device_id_type=MESH)
        return carry

    lax.fori_loop(1, n_clus, greet, 0)

    loads[0].wait()
    loads[1].wait()

    def build(step, carry):
        first = pl.multiple_of(step * 32, 32)
        places = lax.broadcasted_iota(jnp.int32, (32, azimuth), 0) + first
        total = jnp.zeros((32, azimuth), F32)
        for point in range(stencil.shape[0]):
            total = total + jnp.where(stencil[point : point + 1, :] == places, weights[point : point + 1, :], 0.0)
        high, low = halves(total)
        phi_hi[pl.ds(first, 32), :] = high
        phi_lo[pl.ds(first, 32), :] = low
        return carry

    lax.fori_loop(0, columns // 32, build, 0)
    for copy in loads[2:]:
        copy.wait()

    pl.semaphore_wait(barrier, n_clus + 2)
    halos = [
        pltpu.make_async_remote_copy(
            src_ref=child, dst_ref=target, send_sem=halo_send.at[place], recv_sem=halo_recv.at[place],
            device_id=(me, side), device_id_type=MESH,
        )
        for place, (target, side) in enumerate([(below, up), (above, down)])
    ]
    for copy in halos:
        copy.start()
    tilts = [
        pltpu.make_async_remote_copy(
            src_ref=phase, dst_ref=cosine.at[place], send_sem=phase_send.at[place - 1], recv_sem=phase_recv.at[place - 1],
            device_id=peer, device_id_type=MESH,
        )
        for place, peer in ((1, (me, pair)), (2, (near, away)))
    ]
    for copy in tilts:
        copy.start()

    for row in range(rows):
        cosine[0, row] = jnp.cos(phase[row])
        sine[0, row] = jnp.sin(phase[row])

    inner = clusters // n_clus
    spot = lax.broadcasted_iota(jnp.int32, (clusters, clusters), 0)
    lane = lax.broadcasted_iota(jnp.int32, (clusters, clusters), 1)
    order = jnp.where((spot % n_clus) * inner + spot // n_clus == lane, 1.0, 0.0).astype(BF16)
    partner = far[...]
    partner = (partner % inner) * n_clus + partner // inner
    wanted = dot(order, partner.astype(F32).astype(BF16), ((1,), (1,)))
    kinds = dot(order, vec[...].astype(F32).astype(BF16), ((1,), (1,)))
    put_row = lax.broadcasted_iota(jnp.int32, (16, 128), 0)
    put_lane = lax.broadcasted_iota(jnp.int32, (16, 128), 1)
    spread = [[], []]
    for part in range(2):
        total_hi = jnp.zeros((table.shape[0], 128), F32)
        total_lo = jnp.zeros((table.shape[0], 128), F32)
        for row in range(rows):
            put = jnp.where(put_row + 16 * row == put_lane, 1.0, 0.0).astype(BF16)
            high, low = halves(table[:, row, part, :])
            total_hi = total_hi + dot(high, put, ((1,), (0,)))
            total_lo = total_lo + dot(low, put, ((1,), (0,)))
        spread[0].append(total_hi.astype(BF16))
        spread[1].append(total_lo.astype(BF16))
    t_hi = jnp.concatenate(spread[0], axis=1)
    t_lo = jnp.concatenate(spread[1], axis=1)
    lane_f = lane.astype(F32)
    kind_f = lax.broadcasted_iota(jnp.int32, (clusters, table.shape[0]), 1).astype(F32)
    for link in range(far_count):
        picks[link] = jnp.where(wanted[:, link : link + 1] == lane_f, 1.0, 0.0).astype(BF16)
        chosen = jnp.where(kinds[:, link : link + 1] == kind_f, 1.0, 0.0).astype(BF16)
        operators[link] = dot(chosen, t_hi, ((1,), (0,))) + dot(chosen, t_lo, ((1,), (0,)))

    for copy in halos:
        copy.wait()

    for row in range(rows):
        total = jnp.zeros((64, columns), F32)
        for step in range(9):
            part = (below, child, above)[step // 3][step % 3]
            total = total + theta[row, step] * part
        high, low = halves(total)
        lhs_hi[row * 64 : (row + 1) * 64, :] = high
        lhs_lo[row * 64 : (row + 1) * 64, :] = low

    plane = lax.div(me, 16)
    seat = lax.rem(me, 16)
    half_w = lax.broadcasted_iota(jnp.int32, (8, 256), 0) < 4
    for turn in (2, 1, 3, 0):
        block = lax.rem(plane + turn, 4)
        lanes = pl.ds(pl.multiple_of(block * 256, 256), 256)
        refined = dot3(lhs_hi[...], lhs_lo[...], phi_hi[:, lanes], phi_lo[:, lanes], ((1,), (0,)))
        fields = []
        for row in range(rows):
            straight = jnp.zeros((8, 256), F32)
            crossed = jnp.zeros((8, 256), F32)
            for octant in range(8):
                piece = refined[row * 64 + octant * 8 : row * 64 + octant * 8 + 8]
                straight = straight + piece * cosine[0, row, octant : octant + 1, lanes]
                crossed = crossed + piece * sine[0, row, octant : octant + 1, lanes]
            crossed = pltpu.roll(crossed, 4, 0)
            field = straight + jnp.where(half_w, -crossed, crossed)
            fields += [field[:, :128], field[:, 128:]]
        packed = swap_groups(jnp.stack(fields, axis=0))
        for row in range(rows):
            for side in range(2):
                msg_out[pl.ds(block * 16 + side * 8, 8), row, :] = packed[row * 2 + side]

        def send(step, carry):
            target = block * 16 + lax.rem(seat + step, 16)
            pltpu.make_async_remote_copy(
                src_ref=msg_out.at[target], dst_ref=msg_in.at[me], send_sem=a2a_send, recv_sem=a2a_recv,
                device_id=(target, ring), device_id_type=MESH,
            ).start()
            return carry

        if turn == 0:
            lax.fori_loop(1, 16, send, 0)
        else:
            lax.fori_loop(4, 20, send, 0)

    own = pltpu.make_async_copy(msg_out.at[me], msg_in.at[me], own_sem.at[0])
    own.start()
    own.wait()
    pltpu.make_async_copy(msg_out.at[others], msg_in.at[others], a2a_recv).wait()

    group = lax.broadcasted_iota(jnp.int32, (n_clus, 128), 1) // 16
    arrived = [msg_in[:, row, :] for row in range(rows)]
    gathered = [[], []]
    for part in range(2):
        for place in range(inner):
            total = jnp.zeros((n_clus, 128), F32)
            for row in range(rows):
                shift = 16 * (row - part * inner - place)
                total = jnp.where(group == row, pltpu.roll(arrived[row], shift % 128, 1), total)
            gathered[part].append(total)
    x_hi, x_lo = halves(
        jnp.concatenate([jnp.concatenate(gathered[0], axis=0), jnp.concatenate(gathered[1], axis=0)], axis=1)
    )
    in_re = jnp.zeros((clusters, 128), F32)
    in_im = jnp.zeros((clusters, 128), F32)
    for link in range(far_count):
        pick = picks[link]
        source = dot(pick, x_hi, ((1,), (0,))) + dot(pick, x_lo, ((1,), (0,)))
        s_re, s_im = source[:, :128], source[:, 128:]
        o_re, o_im = operators[link, :, :128], operators[link, :, 128:]
        in_re = in_re + (o_re * s_re - o_im * s_im)
        in_im = in_im + (o_re * s_im + o_im * s_re)
    for row in range(rows):
        total = jnp.zeros((n_clus, 128), F32)
        for part, field in enumerate((in_re, in_im)):
            for place in range(inner):
                spot_of = part * inner + place
                piece = field[place * n_clus : (place + 1) * n_clus]
                total = jnp.where(group == spot_of, pltpu.roll(piece, (16 * (spot_of - row)) % 128, 1), total)
        back_out[:, row, :] = total

    def give(step, carry):
        target = lax.rem(me + step, n_clus)
        pltpu.make_async_remote_copy(
            src_ref=back_out.at[target], dst_ref=back_in.at[me], send_sem=back_send, recv_sem=back_recv,
            device_id=(target, ring), device_id_type=MESH,
        ).start()
        return carry

    lax.fori_loop(1, n_clus, give, 0)
    own = pltpu.make_async_copy(back_out.at[me], back_in.at[me], own_sem.at[1])
    own.start()

    for copy in tilts:
        copy.wait()
    for place in (1, 2):
        for row in range(rows):
            angle = cosine[place, row]
            sine[place, row] = jnp.sin(angle)
            cosine[place, row] = jnp.cos(angle)

    own.wait()
    pltpu.make_async_copy(back_out.at[others], back_in.at[others], back_recv).wait()

    for row in range(rows):
        field = swap_groups(back_in[:, row, :].reshape(n_clus // 8, 8, 128))
        for block in range(n_clus // 8):
            inc_out[row, :, block * 128 : (block + 1) * 128] = field[block]
    passes = [
        pltpu.make_async_remote_copy(
            src_ref=inc_out, dst_ref=target, send_sem=inc_send.at[place], recv_sem=inc_recv.at[place],
            device_id=(me, side), device_id_type=MESH,
        )
        for place, (target, side) in enumerate([(inc_far, away), (inc_pair, pair)])
    ]
    for copy in passes:
        copy.start()

    half = lax.broadcasted_iota(jnp.int32, (8, 128), 0) < 4

    def lower(source, place, base):
        for block in range(azimuth // 128):
            lanes = slice(block * 128, (block + 1) * 128)
            straight = [source[row, :, lanes] for row in range(rows)]
            crossed = []
            for row in range(rows):
                swapped = pltpu.roll(straight[row], 4, 0)
                crossed.append(jnp.where(half, swapped, -swapped))
            scale = [[theta[row, base + step] for step in range(3)] for row in range(rows)]
            for octant in range(0, 8, 2):
                sums = [[], [], []]
                for one in (octant, octant + 1):
                    totals = [jnp.zeros((8, 128), F32)] * 3
                    for row in range(rows):
                        piece = (
                            straight[row] * cosine[place, row, one : one + 1, lanes]
                            + crossed[row] * sine[place, row, one : one + 1, lanes]
                        )
                        totals = [total + scale[row][step] * piece for step, total in enumerate(totals)]
                    for step in range(3):
                        sums[step].append(totals[step])
                for step in range(3):
                    span = slice(step * 64 + octant * 8, step * 64 + octant * 8 + 16)
                    value = jnp.concatenate(sums[step], axis=0)
                    if place > 0:
                        value = value + total_low[span, lanes]
                    if place < 2:
                        total_low[span, lanes] = value
                    else:
                        high, low = halves(value)
                        low_hi[span, lanes] = high
                        low_lo[span, lanes] = low

    lower(inc_out, 0, 3)
    passes[1].wait()
    lower(inc_pair, 1, 6 * core)
    pltpu.make_async_copy(msg_out.at[others], msg_in.at[others], a2a_send).wait()
    pltpu.make_async_copy(back_out.at[others], back_in.at[others], back_send).wait()
    passes[0].wait()
    lower(inc_far, 2, 6 - 6 * core)

    for cut in range(0, columns, 256):
        span = slice(cut, cut + 256)
        narrow = dot3(low_hi[...], low_lo[...], phi_hi[span, :], phi_lo[span, :], ((1,), (1,)))
        for step in range(3):
            child_out[step, :, span] = narrow[step * 64 : (step + 1) * 64]


def per_device(n_clus, n_samp, child_patterns, theta_weights, phi_stencil, phi_weights, shift_phase, translation_table, far_list, far_vector):
    groups = child_patterns.shape[0] // 8
    own_rows, columns = child_patterns.shape[2:]
    rows = theta_weights.shape[0]
    azimuth = phi_stencil.shape[0]
    clusters, far_count = far_list.shape
    child = child_patterns.reshape(groups, 8, 2, own_rows, columns).transpose(3, 1, 2, 0, 4)
    child = child.reshape(own_rows, groups * 16, columns)
    vmem = pl.BlockSpec(memory_space=pltpu.VMEM)
    smem = pl.BlockSpec(memory_space=pltpu.SMEM)
    hbm = pl.BlockSpec(memory_space=pltpu.HBM)
    block = (own_rows, groups * 16, columns)
    field = (rows, 8, azimuth)
    stencil, weights = phi_stencil.T, phi_weights.T
    phase = shift_phase.transpose(1, 0, 2)
    table = translation_table.transpose(0, 2, 1, 3)
    far, vec = far_list.T, far_vector.T
    mail = pltpu.VMEM((n_clus, rows, 128), F32)
    incoming, child_incoming = pl.pallas_call(
        functools.partial(window, n_clus, n_samp),
        out_shape=(jax.ShapeDtypeStruct(field, F32), jax.ShapeDtypeStruct(block, F32)),
        in_specs=[smem, vmem] + [hbm] * 6,
        out_specs=(vmem, vmem),
        scratch_shapes=[
            pltpu.VMEM(stencil.shape, jnp.int32),
            pltpu.VMEM(weights.shape, F32),
            pltpu.VMEM(field, F32),
            pltpu.VMEM(table.shape, F32),
            pltpu.VMEM(far.shape, jnp.int32),
            pltpu.VMEM(vec.shape, jnp.int32),
            pltpu.VMEM((columns, azimuth), BF16),
            pltpu.VMEM((columns, azimuth), BF16),
            pltpu.VMEM((3,) + field, F32),
            pltpu.VMEM((3,) + field, F32),
            pltpu.VMEM((far_count, clusters, clusters), BF16),
            pltpu.VMEM((far_count, clusters, 256), F32),
            pltpu.VMEM(block, F32),
            pltpu.VMEM(block, F32),
            pltpu.VMEM((rows * 64, columns), BF16),
            pltpu.VMEM((rows * 64, columns), BF16),
            pltpu.VMEM((own_rows * 64, azimuth), BF16),
            pltpu.VMEM((own_rows * 64, azimuth), BF16),
            pltpu.VMEM((own_rows * 64, azimuth), F32),
            mail,
            mail,
            mail,
            mail,
            pltpu.VMEM(field, F32),
            pltpu.VMEM(field, F32),
            pltpu.SemaphoreType.DMA((6,)),
            pltpu.SemaphoreType.DMA((2,)),
            pltpu.SemaphoreType.DMA((2,)),
            pltpu.SemaphoreType.DMA((2,)),
            pltpu.SemaphoreType.DMA((2,)),
            pltpu.SemaphoreType.DMA,
            pltpu.SemaphoreType.DMA,
            pltpu.SemaphoreType.DMA((2,)),
            pltpu.SemaphoreType.DMA,
            pltpu.SemaphoreType.DMA,
            pltpu.SemaphoreType.DMA((2,)),
            pltpu.SemaphoreType.DMA((2,)),
        ],
        compiler_params=pltpu.CompilerParams(collective_id=0, has_side_effects=True, vmem_limit_bytes=48 << 20),
    )(theta_weights, child, stencil, weights, phase, table, far, vec)
    incoming = incoming.reshape(rows, 2, groups, azimuth).transpose(2, 1, 0, 3)
    child_incoming = child_incoming.reshape(own_rows, 8, 2, groups, columns).transpose(3, 1, 2, 0, 4)
    return incoming, child_incoming.reshape(child_patterns.shape)


def solution(mesh):
    placed = (
        P("clus", None, "samp", None),
        P(),
        P(),
        P(),
        P(None, "samp", None),
        P(None, None, "samp", "clus"),
        P(),
        P(),
    )
    return jax.shard_map(
        functools.partial(per_device, mesh.shape["clus"], mesh.shape["samp"]),
        mesh=mesh,
        in_specs=placed,
        out_specs=(P("clus", None, "samp", None), P("clus", None, "samp", None)),
        check_vma=False,
    )
```

```python
import functools

import jax
import jax.numpy as jnp
from jax import lax
from jax.experimental import pallas as pl
from jax.experimental.pallas import tpu as pltpu
from jax.sharding import PartitionSpec as P

MESH = pl.DeviceIdType.MESH
F32 = jnp.float32
BF16 = jnp.bfloat16


def halves(value):
    high = value.astype(BF16)
    return high, (value - high.astype(F32)).astype(BF16)


def dot(a, b, contract):
    return lax.dot_general(a, b, ((contract[0], contract[1]), ((), ())), preferred_element_type=F32)


def dot3(a_hi, a_lo, b_hi, b_lo, contract):
    return dot(a_hi, b_hi, contract) + (dot(a_hi, b_lo, contract) + dot(a_lo, b_hi, contract))


def swap_groups(value):
    row = lax.broadcasted_iota(jnp.int32, (8, 128), 0)
    group = lax.broadcasted_iota(jnp.int32, (8, 128), 1) // 16
    for bit in (4, 2, 1):
        own, other = (row // bit) % 2, (group // bit) % 2
        rise = pltpu.roll(pltpu.roll(value, 8 - bit, 1), 16 * bit, 2)
        fall = rise if bit == 4 else pltpu.roll(pltpu.roll(value, bit, 1), 128 - 16 * bit, 2)
        value = jnp.where((own == other)[None], value, jnp.where((own < other)[None], rise, fall))
    return value


def window(
    n_clus, n_samp,
    theta, child, stencil_in, weights_in, phase_in, table_in, far_in, vec_in,
    inc_out, child_out,
    stencil, weights, phase, table, far, vec,
    phi_hi, phi_lo, cosine, sine, picks, operators,
    below, above, lhs_hi, lhs_lo, low_hi, low_lo, total_low,
    msg_out, msg_in, back_out, back_in, inc_pair, inc_far,
    in_sem, halo_send, halo_recv, phase_send, phase_recv,
    a2a_send, a2a_recv, own_sem, back_send, back_recv, inc_send, inc_recv, zone,
):
    me = lax.axis_index("clus")
    ring = lax.axis_index("samp")
    up = lax.rem(ring + 1, n_samp)
    down = lax.rem(ring + n_samp - 1, n_samp)
    core = lax.rem(ring, 2)
    pair = ring + 1 - 2 * core
    away = lax.rem(ring + n_samp - 1 + 2 * core, n_samp)
    deep = lax.rem(lax.div(me, 4), 4)
    first_end = jnp.where(ring == 0, 3, 0)
    last_end = jnp.where(ring == n_samp - 1, 1, 0)
    near = me + 4 * (lax.rem(deep + first_end + last_end, 4) - deep)
    columns = child.shape[2]
    azimuth = stencil.shape[1]
    rows = phase.shape[0]
    far_count, clusters = far.shape
    others = pl.ds(0, n_clus - 1)

    loads = [
        pltpu.make_async_copy(source, target, in_sem.at[place])
        for place, (source, target) in enumerate(
            [(stencil_in, stencil), (weights_in, weights), (phase_in, phase), (table_in, table), (far_in, far), (vec_in, vec)]
        )
    ]
    barrier = pltpu.get_barrier_semaphore()
    layers = [(me + 4 * (lax.rem(deep + by, 4) - deep), ring) for by in (1, 3)]
    for peer in [(me, up), (me, down), (near, away)] + layers:
        pl.semaphore_signal(barrier, inc=1, device_id=peer, device_id_type=MESH)
    plane = lax.div(me, 16)
    across = lax.rem(me, 4)

    def greet(step, carry):
        peer = lax.rem(plane + lax.div(step, 4), 4) * 16 + deep * 4 + lax.rem(across + lax.rem(step, 4), 4)
        pl.semaphore_signal(barrier, inc=1, device_id=(peer, ring), device_id_type=MESH)
        return carry

    lax.fori_loop(1, 16, greet, 0)
    for copy in loads:
        copy.start()

    def tell(stage):
        for peer in layers:
            pl.semaphore_signal(zone.at[stage], inc=1, device_id=peer, device_id_type=MESH)

    loads[2].wait()
    pl.semaphore_wait(barrier, 20)
    halos = [
        pltpu.make_async_remote_copy(
            src_ref=child, dst_ref=target, send_sem=halo_send.at[place], recv_sem=halo_recv.at[place],
            device_id=(me, side), device_id_type=MESH,
        )
        for place, (target, side) in enumerate([(below, up), (above, down)])
    ]
    for copy in halos:
        copy.start()
    tilts = [
        pltpu.make_async_remote_copy(
            src_ref=phase, dst_ref=cosine.at[place], send_sem=phase_send.at[place - 1], recv_sem=phase_recv.at[place - 1],
            device_id=peer, device_id_type=MESH,
        )
        for place, peer in ((1, (me, pair)), (2, (near, away)))
    ]
    for copy in tilts:
        copy.start()
    tell(0)

    for row in range(rows):
        cosine[0, row] = jnp.cos(phase[row])
        sine[0, row] = jnp.sin(phase[row])

    pl.semaphore_wait(zone.at[0], 2)
    tell(1)
    loads[0].wait()
    loads[1].wait()

    def build(step, carry):
        first = pl.multiple_of(step * 32, 32)
        places = lax.broadcasted_iota(jnp.int32, (32, azimuth), 0) + first
        total = jnp.zeros((32, azimuth), F32)
        for point in range(stencil.shape[0]):
            total = total + jnp.where(stencil[point : point + 1, :] == places, weights[point : point + 1, :], 0.0)
        high, low = halves(total)
        phi_hi[pl.ds(first, 32), :] = high
        phi_lo[pl.ds(first, 32), :] = low
        return carry

    lax.fori_loop(0, columns // 32, build, 0)
    for copy in loads[3:]:
        copy.wait()

    inner = clusters // n_clus
    spot = lax.broadcasted_iota(jnp.int32, (clusters, clusters), 0)
    lane = lax.broadcasted_iota(jnp.int32, (clusters, clusters), 1)
    named = ((spot // 64) * 16 + spot % 16) * inner + (spot // 16) % inner
    order = jnp.where(named == lane, 1.0, 0.0).astype(BF16)
    partner = far[...]
    partner = (partner % inner) * n_clus + partner // inner
    wanted = dot(order, partner.astype(F32).astype(BF16), ((1,), (1,)))
    kinds = dot(order, vec[...].astype(F32).astype(BF16), ((1,), (1,)))
    put_row = lax.broadcasted_iota(jnp.int32, (16, 128), 0)
    put_lane = lax.broadcasted_iota(jnp.int32, (16, 128), 1)
    spread = [[], []]
    for part in range(2):
        total_hi = jnp.zeros((table.shape[0], 128), F32)
        total_lo = jnp.zeros((table.shape[0], 128), F32)
        for row in range(rows):
            put = jnp.where(put_row + 16 * row == put_lane, 1.0, 0.0).astype(BF16)
            high, low = halves(table[:, row, part, :])
            total_hi = total_hi + dot(high, put, ((1,), (0,)))
            total_lo = total_lo + dot(low, put, ((1,), (0,)))
        spread[0].append(total_hi.astype(BF16))
        spread[1].append(total_lo.astype(BF16))
    t_hi = jnp.concatenate(spread[0], axis=1)
    t_lo = jnp.concatenate(spread[1], axis=1)
    lane_f = lane.astype(F32)
    kind_f = lax.broadcasted_iota(jnp.int32, (clusters, table.shape[0]), 1).astype(F32)
    for link in range(far_count):
        pick = jnp.where(wanted[:, link : link + 1] == lane_f, 1.0, 0.0).astype(BF16)
        chosen = jnp.where(kinds[:, link : link + 1] == kind_f, 1.0, 0.0).astype(BF16)
        operator = dot(chosen, t_hi, ((1,), (0,))) + dot(chosen, t_lo, ((1,), (0,)))
        for part in range(4):
            picks[part, link * 64 : (link + 1) * 64, :] = pick[part * 64 : (part + 1) * 64]
            operators[part, link * 64 : (link + 1) * 64, :] = operator[part * 64 : (part + 1) * 64]

    for copy in halos:
        copy.wait()

    for row in range(rows):
        total = jnp.zeros((64, columns), F32)
        for step in range(9):
            part = (below, child, above)[step // 3][step % 3]
            total = total + theta[row, step] * part
        high, low = halves(total)
        lhs_hi[row * 64 : (row + 1) * 64, :] = high
        lhs_lo[row * 64 : (row + 1) * 64, :] = low

    pl.semaphore_wait(zone.at[1], 2)
    seat = lax.rem(me, 16)
    half_w = lax.broadcasted_iota(jnp.int32, (8, 256), 0) < 4
    turns = (2, 1, 3, 0)

    def mail_plane(turn, outbox, inbox, send_sem, recv_sem):
        block = lax.rem(plane + turn, 4)

        def send(step, carry):
            target = block * 16 + lax.rem(seat + step, 16)
            pltpu.make_async_remote_copy(
                src_ref=outbox.at[target], dst_ref=inbox.at[me], send_sem=send_sem, recv_sem=recv_sem,
                device_id=(target, ring), device_id_type=MESH,
            ).start()
            return carry

        if turn == 0:
            lax.fori_loop(1, 16, send, 0)
        else:
            lax.fori_loop(4, 20, send, 0)

    def spans(turn):
        return pl.ds(pl.multiple_of(lax.rem(plane + turn, 4) * 256, 256), 256)

    def refine(turn):
        lanes = spans(turn)
        return dot3(lhs_hi[...], lhs_lo[...], phi_hi[:, lanes], phi_lo[:, lanes], ((1,), (0,)))

    refined = refine(turns[0])
    for place, turn in enumerate(turns):
        block = lax.rem(plane + turn, 4)
        lanes = spans(turn)
        following = refine(turns[place + 1]) if place < 3 else None
        fields = []
        for row in range(rows):
            straight = jnp.zeros((8, 256), F32)
            crossed = jnp.zeros((8, 256), F32)
            for octant in range(8):
                piece = refined[row * 64 + octant * 8 : row * 64 + octant * 8 + 8]
                straight = straight + piece * cosine[0, row, octant : octant + 1, lanes]
                crossed = crossed + piece * sine[0, row, octant : octant + 1, lanes]
            crossed = pltpu.roll(crossed, 4, 0)
            field = straight + jnp.where(half_w, -crossed, crossed)
            fields += [field[:, :128], field[:, 128:]]
        packed = swap_groups(jnp.stack(fields, axis=0))
        for row in range(rows):
            for side in range(2):
                msg_out[pl.ds(block * 16 + side * 8, 8), row, :] = packed[row * 2 + side]
        mail_plane(turn, msg_out, msg_in, a2a_send, a2a_recv)
        refined = following

    own = pltpu.make_async_copy(msg_out.at[me], msg_in.at[me], own_sem.at[0])
    own.start()
    own.wait()
    pltpu.make_async_copy(msg_out.at[others], msg_in.at[others], a2a_recv).wait()

    group = lax.broadcasted_iota(jnp.int32, (n_clus, 128), 1) // 16
    arrived = [msg_in[:, row, :] for row in range(rows)]
    gathered = [[], []]
    for part in range(2):
        for place in range(inner):
            total = jnp.zeros((n_clus, 128), F32)
            for row in range(rows):
                shift = 16 * (row - part * inner - place)
                total = jnp.where(group == row, pltpu.roll(arrived[row], shift % 128, 1), total)
            gathered[part].append(total)
    x_hi, x_lo = halves(
        jnp.concatenate([jnp.concatenate(gathered[0], axis=0), jnp.concatenate(gathered[1], axis=0)], axis=1)
    )
    group = lax.broadcasted_iota(jnp.int32, (16, 128), 1) // 16

    def fetch(turn):
        pick = picks[lax.rem(plane + turn, 4)]
        return dot(pick, x_hi, ((1,), (0,))) + dot(pick, x_lo, ((1,), (0,)))

    source = fetch(turns[0])
    for place, turn in enumerate(turns):
        block = lax.rem(plane + turn, 4)
        following = fetch(turns[place + 1]) if place < 3 else None
        in_re = jnp.zeros((64, 128), F32)
        in_im = jnp.zeros((64, 128), F32)
        for link in range(far_count):
            span = slice(link * 64, (link + 1) * 64)
            s_re, s_im = source[span, :128], source[span, 128:]
            o_re, o_im = operators[block, span, :128], operators[block, span, 128:]
            in_re = in_re + (o_re * s_re - o_im * s_im)
            in_im = in_im + (o_re * s_im + o_im * s_re)
        for row in range(rows):
            total = jnp.zeros((16, 128), F32)
            for part, field in enumerate((in_re, in_im)):
                for seat_in in range(inner):
                    spot_of = part * inner + seat_in
                    piece = field[seat_in * 16 : (seat_in + 1) * 16]
                    total = jnp.where(group == spot_of, pltpu.roll(piece, (16 * (spot_of - row)) % 128, 1), total)
            back_out[pl.ds(block * 16, 16), row, :] = total
        mail_plane(turn, back_out, back_in, back_send, back_recv)
        source = following

    own = pltpu.make_async_copy(back_out.at[me], back_in.at[me], own_sem.at[1])
    own.start()

    for copy in tilts:
        copy.wait()
    for place in (1, 2):
        for row in range(rows):
            angle = cosine[place, row]
            sine[place, row] = jnp.sin(angle)
            cosine[place, row] = jnp.cos(angle)

    own.wait()
    pltpu.make_async_copy(back_out.at[others], back_in.at[others], back_recv).wait()

    for row in range(rows):
        field = swap_groups(back_in[:, row, :].reshape(n_clus // 8, 8, 128))
        for block in range(n_clus // 8):
            inc_out[row, :, block * 128 : (block + 1) * 128] = field[block]
    wide = azimuth // 2
    passes = [
        pltpu.make_async_remote_copy(
            src_ref=origin, dst_ref=target, send_sem=inc_send.at[place], recv_sem=inc_recv.at[place],
            device_id=(me, side), device_id_type=MESH,
        )
        for place, (origin, target, side) in enumerate(
            [
                (inc_out.at[:, :, pl.ds(0, wide)], inc_far.at[:, :, pl.ds(0, wide)], away),
                (inc_out.at[:, :, pl.ds(wide, wide)], inc_far.at[:, :, pl.ds(wide, wide)], away),
                (inc_out, inc_pair, pair),
            ]
        )
    ]
    for copy in passes:
        copy.start()

    half = lax.broadcasted_iota(jnp.int32, (8, 128), 0) < 4

    def lower(source, place, base, blocks):
        for block in blocks:
            lanes = slice(block * 128, (block + 1) * 128)
            straight = [source[row, :, lanes] for row in range(rows)]
            crossed = []
            for row in range(rows):
                swapped = pltpu.roll(straight[row], 4, 0)
                crossed.append(jnp.where(half, swapped, -swapped))
            scale = [[theta[row, base + step] for step in range(3)] for row in range(rows)]
            for octant in range(0, 8, 2):
                sums = [[], [], []]
                for one in (octant, octant + 1):
                    totals = [jnp.zeros((8, 128), F32)] * 3
                    for row in range(rows):
                        piece = (
                            straight[row] * cosine[place, row, one : one + 1, lanes]
                            + crossed[row] * sine[place, row, one : one + 1, lanes]
                        )
                        totals = [total + scale[row][step] * piece for step, total in enumerate(totals)]
                    for step in range(3):
                        sums[step].append(totals[step])
                for step in range(3):
                    span = slice(step * 64 + octant * 8, step * 64 + octant * 8 + 16)
                    value = jnp.concatenate(sums[step], axis=0)
                    if place > 0:
                        value = value + total_low[span, lanes]
                    if place < 2:
                        total_low[span, lanes] = value
                    else:
                        high, low = halves(value)
                        low_hi[span, lanes] = high
                        low_lo[span, lanes] = low

    blocks = azimuth // 128
    lower(inc_out, 0, 3, range(blocks))
    passes[2].wait()
    lower(inc_pair, 1, 6 * core, range(blocks))
    pltpu.make_async_copy(msg_out.at[others], msg_in.at[others], a2a_send).wait()
    pltpu.make_async_copy(back_out.at[others], back_in.at[others], back_send).wait()
    for part in range(2):
        passes[part].wait()
        lower(inc_far, 2, 6 - 6 * core, range(part * blocks // 2, (part + 1) * blocks // 2))
        lanes = slice(part * wide, (part + 1) * wide)
        for cut in range(0, columns, 256):
            span = slice(cut, cut + 256)
            narrow = dot3(low_hi[:, lanes], low_lo[:, lanes], phi_hi[span, lanes], phi_lo[span, lanes], ((1,), (1,)))
            for step in range(3):
                value = narrow[step * 64 : (step + 1) * 64]
                child_out[step, :, span] = value if part == 0 else child_out[step, :, span] + value


def per_device(n_clus, n_samp, child_patterns, theta_weights, phi_stencil, phi_weights, shift_phase, translation_table, far_list, far_vector):
    groups = child_patterns.shape[0] // 8
    own_rows, columns = child_patterns.shape[2:]
    rows = theta_weights.shape[0]
    azimuth = phi_stencil.shape[0]
    clusters, far_count = far_list.shape
    child = child_patterns.reshape(groups, 8, 2, own_rows, columns).transpose(3, 1, 2, 0, 4)
    child = child.reshape(own_rows, groups * 16, columns)
    vmem = pl.BlockSpec(memory_space=pltpu.VMEM)
    smem = pl.BlockSpec(memory_space=pltpu.SMEM)
    hbm = pl.BlockSpec(memory_space=pltpu.HBM)
    block = (own_rows, groups * 16, columns)
    field = (rows, 8, azimuth)
    stencil, weights = phi_stencil.T, phi_weights.T
    phase = shift_phase.transpose(1, 0, 2)
    table = translation_table.transpose(0, 2, 1, 3)
    far, vec = far_list.T, far_vector.T
    mail = pltpu.VMEM((n_clus, rows, 128), F32)
    incoming, child_incoming = pl.pallas_call(
        functools.partial(window, n_clus, n_samp),
        out_shape=(jax.ShapeDtypeStruct(field, F32), jax.ShapeDtypeStruct(block, F32)),
        in_specs=[smem, vmem] + [hbm] * 6,
        out_specs=(vmem, vmem),
        scratch_shapes=[
            pltpu.VMEM(stencil.shape, jnp.int32),
            pltpu.VMEM(weights.shape, F32),
            pltpu.VMEM(field, F32),
            pltpu.VMEM(table.shape, F32),
            pltpu.VMEM(far.shape, jnp.int32),
            pltpu.VMEM(vec.shape, jnp.int32),
            pltpu.VMEM((columns, azimuth), BF16),
            pltpu.VMEM((columns, azimuth), BF16),
            pltpu.VMEM((3,) + field, F32),
            pltpu.VMEM((3,) + field, F32),
            pltpu.VMEM((4, far_count * 64, clusters), BF16),
            pltpu.VMEM((4, far_count * 64, 256), F32),
            pltpu.VMEM(block, F32),
            pltpu.VMEM(block, F32),
            pltpu.VMEM((rows * 64, columns), BF16),
            pltpu.VMEM((rows * 64, columns), BF16),
            pltpu.VMEM((own_rows * 64, azimuth), BF16),
            pltpu.VMEM((own_rows * 64, azimuth), BF16),
            pltpu.VMEM((own_rows * 64, azimuth), F32),
            mail,
            mail,
            mail,
            mail,
            pltpu.VMEM(field, F32),
            pltpu.VMEM(field, F32),
            pltpu.SemaphoreType.DMA((6,)),
            pltpu.SemaphoreType.DMA((2,)),
            pltpu.SemaphoreType.DMA((2,)),
            pltpu.SemaphoreType.DMA((2,)),
            pltpu.SemaphoreType.DMA((2,)),
            pltpu.SemaphoreType.DMA,
            pltpu.SemaphoreType.DMA,
            pltpu.SemaphoreType.DMA((2,)),
            pltpu.SemaphoreType.DMA,
            pltpu.SemaphoreType.DMA,
            pltpu.SemaphoreType.DMA((3,)),
            pltpu.SemaphoreType.DMA((3,)),
            pltpu.SemaphoreType.REGULAR((2,)),
        ],
        compiler_params=pltpu.CompilerParams(collective_id=0, has_side_effects=True, vmem_limit_bytes=48 << 20),
    )(theta_weights, child, stencil, weights, phase, table, far, vec)
    incoming = incoming.reshape(rows, 2, groups, azimuth).transpose(2, 1, 0, 3)
    child_incoming = child_incoming.reshape(own_rows, 8, 2, groups, columns).transpose(3, 1, 2, 0, 4)
    return incoming, child_incoming.reshape(child_patterns.shape)


def solution(mesh):
    placed = (
        P("clus", None, "samp", None),
        P(),
        P(),
        P(),
        P(None, "samp", None),
        P(None, None, "samp", "clus"),
        P(),
        P(),
    )
    return jax.shard_map(
        functools.partial(per_device, mesh.shape["clus"], mesh.shape["samp"]),
        mesh=mesh,
        in_specs=placed,
        out_specs=(P("clus", None, "samp", None), P("clus", None, "samp", None)),
        check_vma=False,
    )
```

```python
import functools

import jax
import jax.numpy as jnp
from jax import lax
from jax.experimental import pallas as pl
from jax.experimental.pallas import tpu as pltpu
from jax.sharding import PartitionSpec as P

MESH = pl.DeviceIdType.MESH
F32 = jnp.float32
BF16 = jnp.bfloat16


def halves(value):
    high = value.astype(BF16)
    return high, (value - high.astype(F32)).astype(BF16)


def dot(a, b, contract):
    return lax.dot_general(a, b, ((contract[0], contract[1]), ((), ())), preferred_element_type=F32)


def dot3(a_hi, a_lo, b_hi, b_lo, contract):
    return dot(a_hi, b_hi, contract) + (dot(a_hi, b_lo, contract) + dot(a_lo, b_hi, contract))


def swap_groups(value):
    row = lax.broadcasted_iota(jnp.int32, (8, 128), 0)
    group = lax.broadcasted_iota(jnp.int32, (8, 128), 1) // 16
    for bit in (4, 2, 1):
        own, other = (row // bit) % 2, (group // bit) % 2
        rise = pltpu.roll(pltpu.roll(value, 8 - bit, 1), 16 * bit, 2)
        fall = rise if bit == 4 else pltpu.roll(pltpu.roll(value, bit, 1), 128 - 16 * bit, 2)
        value = jnp.where((own == other)[None], value, jnp.where((own < other)[None], rise, fall))
    return value


def window(
    n_clus, n_samp,
    theta, child, stencil_in, weights_in, phase_in, table_in, far_in, vec_in,
    inc_out, child_out,
    stencil, weights, phase, table, far, vec,
    phi_hi, phi_lo, cosine, sine, picks, operators,
    below, above, lhs_hi, lhs_lo, low_hi, low_lo, total_low,
    msg_out, msg_in, back_out, back_in, inc_pair, inc_far,
    in_sem, halo_send, halo_recv, phase_send, phase_recv,
    a2a_send, a2a_recv, own_sem, back_send, back_recv, inc_send, inc_recv, zone,
):
    me = lax.axis_index("clus")
    ring = lax.axis_index("samp")
    up = lax.rem(ring + 1, n_samp)
    down = lax.rem(ring + n_samp - 1, n_samp)
    core = lax.rem(ring, 2)
    pair = ring + 1 - 2 * core
    away = lax.rem(ring + n_samp - 1 + 2 * core, n_samp)
    deep = lax.rem(lax.div(me, 4), 4)
    first_end = jnp.where(ring == 0, 3, 0)
    last_end = jnp.where(ring == n_samp - 1, 1, 0)
    near = me + 4 * (lax.rem(deep + first_end + last_end, 4) - deep)
    columns = child.shape[2]
    azimuth = stencil.shape[1]
    rows = phase.shape[0]
    some = rows // 2
    far_count, clusters = far.shape
    others = pl.ds(0, n_clus - 1)

    loads = [
        pltpu.make_async_copy(source, target, in_sem.at[place])
        for place, (source, target) in enumerate(
            [(stencil_in, stencil), (weights_in, weights), (phase_in, phase), (table_in, table), (far_in, far), (vec_in, vec)]
        )
    ]
    barrier = pltpu.get_barrier_semaphore()
    layers = [(me + 4 * (lax.rem(deep + by, 4) - deep), ring) for by in (1, 3)]
    for peer in [(me, up), (me, down), (near, away)] + layers:
        pl.semaphore_signal(barrier, inc=1, device_id=peer, device_id_type=MESH)
    plane = lax.div(me, 16)
    across = lax.rem(me, 4)

    def greet(step, carry):
        peer = lax.rem(plane + lax.div(step, 4), 4) * 16 + deep * 4 + lax.rem(across + lax.rem(step, 4), 4)
        pl.semaphore_signal(barrier, inc=1, device_id=(peer, ring), device_id_type=MESH)
        return carry

    lax.fori_loop(1, 16, greet, 0)
    for copy in loads:
        copy.start()

    def tell(stage):
        for peer in layers:
            pl.semaphore_signal(zone.at[stage], inc=1, device_id=peer, device_id_type=MESH)

    loads[2].wait()
    pl.semaphore_wait(barrier, 20)
    halos = [
        pltpu.make_async_remote_copy(
            src_ref=child, dst_ref=target, send_sem=halo_send.at[place], recv_sem=halo_recv.at[place],
            device_id=(me, side), device_id_type=MESH,
        )
        for place, (target, side) in enumerate([(below, up), (above, down)])
    ]
    for copy in halos:
        copy.start()
    tilts = [
        pltpu.make_async_remote_copy(
            src_ref=phase, dst_ref=cosine.at[place], send_sem=phase_send.at[place - 1], recv_sem=phase_recv.at[place - 1],
            device_id=peer, device_id_type=MESH,
        )
        for place, peer in ((1, (me, pair)), (2, (near, away)))
    ]
    for copy in tilts:
        copy.start()
    tell(0)

    for row in range(rows):
        cosine[0, row] = jnp.cos(phase[row])
        sine[0, row] = jnp.sin(phase[row])

    pl.semaphore_wait(zone.at[0], 2)
    tell(1)
    loads[0].wait()
    loads[1].wait()

    def build(step, carry):
        first = pl.multiple_of(step * 32, 32)
        places = lax.broadcasted_iota(jnp.int32, (32, azimuth), 0) + first
        total = jnp.zeros((32, azimuth), F32)
        for point in range(stencil.shape[0]):
            total = total + jnp.where(stencil[point : point + 1, :] == places, weights[point : point + 1, :], 0.0)
        high, low = halves(total)
        phi_hi[pl.ds(first, 32), :] = high
        phi_lo[pl.ds(first, 32), :] = low
        return carry

    lax.fori_loop(0, columns // 32, build, 0)
    for copy in loads[3:]:
        copy.wait()

    inner = clusters // n_clus
    spot = lax.broadcasted_iota(jnp.int32, (clusters, clusters), 0)
    lane = lax.broadcasted_iota(jnp.int32, (clusters, clusters), 1)
    named = ((spot // 64) * 16 + spot % 16) * inner + (spot // 16) % inner
    order = jnp.where(named == lane, 1.0, 0.0).astype(BF16)
    partner = far[...]
    partner = (partner % inner) * n_clus + partner // inner
    wanted = dot(order, partner.astype(F32).astype(BF16), ((1,), (1,)))
    kinds = dot(order, vec[...].astype(F32).astype(BF16), ((1,), (1,)))
    put_row = lax.broadcasted_iota(jnp.int32, (16, 128), 0)
    put_lane = lax.broadcasted_iota(jnp.int32, (16, 128), 1)
    tables = []
    for side in range(2):
        total_hi = jnp.zeros((table.shape[0], 128), F32)
        total_lo = jnp.zeros((table.shape[0], 128), F32)
        for row in range(some):
            for part in range(2):
                put = jnp.where(put_row + (64 * part + 16 * row) == put_lane, 1.0, 0.0).astype(BF16)
                high, low = halves(table[:, side * some + row, part, :])
                total_hi = total_hi + dot(high, put, ((1,), (0,)))
                total_lo = total_lo + dot(low, put, ((1,), (0,)))
        tables.append((total_hi.astype(BF16), total_lo.astype(BF16)))
    lane_f = lane.astype(F32)
    kind_f = lax.broadcasted_iota(jnp.int32, (clusters, table.shape[0]), 1).astype(F32)
    for link in range(far_count):
        pick = jnp.where(wanted[:, link : link + 1] == lane_f, 1.0, 0.0).astype(BF16)
        chosen = jnp.where(kinds[:, link : link + 1] == kind_f, 1.0, 0.0).astype(BF16)
        for part in range(4):
            picks[part, link * 64 : (link + 1) * 64, :] = pick[part * 64 : (part + 1) * 64]
        for side, (t_hi, t_lo) in enumerate(tables):
            operator = dot(chosen, t_hi, ((1,), (0,))) + dot(chosen, t_lo, ((1,), (0,)))
            for part in range(4):
                operators[side, part, link * 64 : (link + 1) * 64, :] = operator[part * 64 : (part + 1) * 64]

    for copy in halos:
        copy.wait()

    for row in range(rows):
        total = jnp.zeros((64, columns), F32)
        for step in range(9):
            part = (below, child, above)[step // 3][step % 3]
            total = total + theta[row, step] * part
        high, low = halves(total)
        lhs_hi[row * 64 : (row + 1) * 64, :] = high
        lhs_lo[row * 64 : (row + 1) * 64, :] = low

    pl.semaphore_wait(zone.at[1], 2)
    seat = lax.rem(me, 16)
    half_w = lax.broadcasted_iota(jnp.int32, (8, 256), 0) < 4
    turns = (2, 1, 3, 0)

    def mail_plane(turn, outbox, inbox, send_sem, recv_sem):
        block = lax.rem(plane + turn, 4)

        def send(step, carry):
            target = block * 16 + lax.rem(seat + step, 16)
            pltpu.make_async_remote_copy(
                src_ref=outbox.at[target], dst_ref=inbox.at[me], send_sem=send_sem, recv_sem=recv_sem,
                device_id=(target, ring), device_id_type=MESH,
            ).start()
            return carry

        if turn == 0:
            lax.fori_loop(1, 16, send, 0)
        else:
            lax.fori_loop(4, 20, send, 0)

    def spans(turn):
        return pl.ds(pl.multiple_of(lax.rem(plane + turn, 4) * 256, 256), 256)

    steps = [(side, turn) for side in range(2) for turn in turns]

    def refine(side, turn):
        lanes = spans(turn)
        span = slice(side * some * 64, (side + 1) * some * 64)
        return dot3(lhs_hi[span, :], lhs_lo[span, :], phi_hi[:, lanes], phi_lo[:, lanes], ((1,), (0,)))

    refined = refine(*steps[0])
    for place, (side, turn) in enumerate(steps):
        block = lax.rem(plane + turn, 4)
        lanes = spans(turn)
        following = refine(*steps[place + 1]) if place + 1 < len(steps) else None
        fields = []
        for row in range(some):
            straight = jnp.zeros((8, 256), F32)
            crossed = jnp.zeros((8, 256), F32)
            for octant in range(8):
                piece = refined[row * 64 + octant * 8 : row * 64 + octant * 8 + 8]
                straight = straight + piece * cosine[0, side * some + row, octant : octant + 1, lanes]
                crossed = crossed + piece * sine[0, side * some + row, octant : octant + 1, lanes]
            crossed = pltpu.roll(crossed, 4, 0)
            field = straight + jnp.where(half_w, -crossed, crossed)
            fields += [field[:, :128], field[:, 128:]]
        packed = swap_groups(jnp.stack(fields, axis=0))
        for row in range(some):
            for part in range(2):
                msg_out[side, pl.ds(block * 16 + part * 8, 8), row, :] = packed[row * 2 + part]
        mail_plane(turn, msg_out.at[side], msg_in.at[side], a2a_send.at[side], a2a_recv.at[side])
        refined = following

    owns = []
    for side in range(2):
        own = pltpu.make_async_copy(msg_out.at[side, me], msg_in.at[side, me], own_sem.at[side])
        own.start()
        owns.append(own)
    group = lax.broadcasted_iota(jnp.int32, (n_clus, 128), 1) // 16 % 4
    small = lax.broadcasted_iota(jnp.int32, (16, 128), 1) // 16 % 4
    real = lax.broadcasted_iota(jnp.int32, (64, 128), 1) < 64
    for side in range(2):
        owns[side].wait()
        pltpu.make_async_copy(msg_out.at[side, others], msg_in.at[side, others], a2a_recv.at[side]).wait()
        arrived = [msg_in[side, :, row, :] for row in range(some)]
        gathered = []
        for seat_in in range(inner):
            total = jnp.zeros((n_clus, 128), F32)
            for row in range(some):
                total = jnp.where(group == row, pltpu.roll(arrived[row], (16 * (row - seat_in)) % 128, 1), total)
            gathered.append(total)
        x_hi, x_lo = halves(jnp.concatenate(gathered, axis=0))

        def fetch(turn):
            pick = picks[lax.rem(plane + turn, 4)]
            return dot(pick, x_hi, ((1,), (0,))) + dot(pick, x_lo, ((1,), (0,)))

        source = fetch(turns[0])
        for place, turn in enumerate(turns):
            block = lax.rem(plane + turn, 4)
            following = fetch(turns[place + 1]) if place < 3 else None
            alike = jnp.zeros((64, 128), F32)
            mixed = jnp.zeros((64, 128), F32)
            for link in range(far_count):
                span = slice(link * 64, (link + 1) * 64)
                piece = source[span]
                operator = operators[side, block, span, :]
                alike = alike + operator * piece
                mixed = mixed + operator * pltpu.roll(piece, 64, 1)
            field = jnp.where(real, alike - pltpu.roll(alike, 64, 1), mixed + pltpu.roll(mixed, 64, 1))
            for row in range(some):
                total = jnp.zeros((16, 128), F32)
                for seat_in in range(inner):
                    piece = field[seat_in * 16 : (seat_in + 1) * 16]
                    total = jnp.where(small == seat_in, pltpu.roll(piece, (16 * (seat_in - row)) % 128, 1), total)
                back_out[side, pl.ds(block * 16, 16), row, :] = total
            mail_plane(turn, back_out.at[side], back_in.at[side], back_send.at[side], back_recv.at[side])
            source = following

    owns = []
    for side in range(2):
        own = pltpu.make_async_copy(back_out.at[side, me], back_in.at[side, me], own_sem.at[2 + side])
        own.start()
        owns.append(own)

    for copy in tilts:
        copy.wait()
    for place in (1, 2):
        for row in range(rows):
            angle = cosine[place, row]
            sine[place, row] = jnp.sin(angle)
            cosine[place, row] = jnp.cos(angle)

    half = lax.broadcasted_iota(jnp.int32, (8, 128), 0) < 4

    def lower(source, place, base, side, blocks):
        last = place == 2 and side == 1
        span_rows = range(side * some, (side + 1) * some)
        scale = [[theta[row, base + step] for step in range(3)] for row in span_rows]
        for block in blocks:
            lanes = slice(block * 128, (block + 1) * 128)
            straight = [source[row, :, lanes] for row in span_rows]
            crossed = []
            for field in straight:
                swapped = pltpu.roll(field, 4, 0)
                crossed.append(jnp.where(half, swapped, -swapped))
            for octant in range(0, 8, 2):
                sums = [[], [], []]
                for one in (octant, octant + 1):
                    totals = [jnp.zeros((8, 128), F32)] * 3
                    for index, row in enumerate(span_rows):
                        piece = (
                            straight[index] * cosine[place, row, one : one + 1, lanes]
                            + crossed[index] * sine[place, row, one : one + 1, lanes]
                        )
                        totals = [total + scale[index][step] * piece for step, total in enumerate(totals)]
                    for step in range(3):
                        sums[step].append(totals[step])
                for step in range(3):
                    span = slice(step * 64 + octant * 8, step * 64 + octant * 8 + 16)
                    value = jnp.concatenate(sums[step], axis=0)
                    if place > 0 or side > 0:
                        value = value + total_low[span, lanes]
                    if not last:
                        total_low[span, lanes] = value
                    else:
                        high, low = halves(value)
                        low_hi[span, lanes] = high
                        low_lo[span, lanes] = low

    blocks = azimuth // 128
    wide = azimuth // 2

    def hand(origin, target, place, side):
        copy = pltpu.make_async_remote_copy(
            src_ref=origin, dst_ref=target, send_sem=inc_send.at[place], recv_sem=inc_recv.at[place],
            device_id=(me, side), device_id_type=MESH,
        )
        copy.start()
        return copy

    passes = []
    for side in range(2):
        owns[side].wait()
        pltpu.make_async_copy(back_out.at[side, others], back_in.at[side, others], back_recv.at[side]).wait()
        for row in range(some):
            field = swap_groups(back_in[side, :, row, :].reshape(n_clus // 8, 8, 128))
            for block in range(blocks):
                inc_out[side * some + row, :, block * 128 : (block + 1) * 128] = field[block]
        span = pl.ds(side * some, some)
        if side == 0:
            passes.append(hand(inc_out.at[span], inc_far.at[span], 0, away))
            passes.append(hand(inc_out.at[span], inc_pair.at[span], 1, pair))
        else:
            for part in range(2):
                cols = pl.ds(part * wide, wide)
                passes.append(hand(inc_out.at[span, :, cols], inc_far.at[span, :, cols], 2 + part, away))
            passes.append(hand(inc_out.at[span], inc_pair.at[span], 4, pair))
        lower(inc_out, 0, 3, side, range(blocks))
    passes[1].wait()
    lower(inc_pair, 1, 6 * core, 0, range(blocks))
    passes[4].wait()
    lower(inc_pair, 1, 6 * core, 1, range(blocks))
    for side in range(2):
        pltpu.make_async_copy(msg_out.at[side, others], msg_in.at[side, others], a2a_send.at[side]).wait()
        pltpu.make_async_copy(back_out.at[side, others], back_in.at[side, others], back_send.at[side]).wait()
    passes[0].wait()
    lower(inc_far, 2, 6 - 6 * core, 0, range(blocks))
    for part in range(2):
        passes[2 + part].wait()
        lower(inc_far, 2, 6 - 6 * core, 1, range(part * blocks // 2, (part + 1) * blocks // 2))
        lanes = slice(part * wide, (part + 1) * wide)
        for cut in range(0, columns, 256):
            span = slice(cut, cut + 256)
            narrow = dot3(low_hi[:, lanes], low_lo[:, lanes], phi_hi[span, lanes], phi_lo[span, lanes], ((1,), (1,)))
            for step in range(3):
                value = narrow[step * 64 : (step + 1) * 64]
                child_out[step, :, span] = value if part == 0 else child_out[step, :, span] + value


def per_device(n_clus, n_samp, child_patterns, theta_weights, phi_stencil, phi_weights, shift_phase, translation_table, far_list, far_vector):
    groups = child_patterns.shape[0] // 8
    own_rows, columns = child_patterns.shape[2:]
    rows = theta_weights.shape[0]
    azimuth = phi_stencil.shape[0]
    clusters, far_count = far_list.shape
    child = child_patterns.reshape(groups, 8, 2, own_rows, columns).transpose(3, 1, 2, 0, 4)
    child = child.reshape(own_rows, groups * 16, columns)
    vmem = pl.BlockSpec(memory_space=pltpu.VMEM)
    smem = pl.BlockSpec(memory_space=pltpu.SMEM)
    hbm = pl.BlockSpec(memory_space=pltpu.HBM)
    block = (own_rows, groups * 16, columns)
    field = (rows, 8, azimuth)
    stencil, weights = phi_stencil.T, phi_weights.T
    phase = shift_phase.transpose(1, 0, 2)
    table = translation_table.transpose(0, 2, 1, 3)
    far, vec = far_list.T, far_vector.T
    mail = pltpu.VMEM((2, n_clus, rows // 2, 128), F32)
    incoming, child_incoming = pl.pallas_call(
        functools.partial(window, n_clus, n_samp),
        out_shape=(jax.ShapeDtypeStruct(field, F32), jax.ShapeDtypeStruct(block, F32)),
        in_specs=[smem, vmem] + [hbm] * 6,
        out_specs=(vmem, vmem),
        scratch_shapes=[
            pltpu.VMEM(stencil.shape, jnp.int32),
            pltpu.VMEM(weights.shape, F32),
            pltpu.VMEM(field, F32),
            pltpu.VMEM(table.shape, F32),
            pltpu.VMEM(far.shape, jnp.int32),
            pltpu.VMEM(vec.shape, jnp.int32),
            pltpu.VMEM((columns, azimuth), BF16),
            pltpu.VMEM((columns, azimuth), BF16),
            pltpu.VMEM((3,) + field, F32),
            pltpu.VMEM((3,) + field, F32),
            pltpu.VMEM((4, far_count * 64, clusters), BF16),
            pltpu.VMEM((2, 4, far_count * 64, 128), F32),
            pltpu.VMEM(block, F32),
            pltpu.VMEM(block, F32),
            pltpu.VMEM((rows * 64, columns), BF16),
            pltpu.VMEM((rows * 64, columns), BF16),
            pltpu.VMEM((own_rows * 64, azimuth), BF16),
            pltpu.VMEM((own_rows * 64, azimuth), BF16),
            pltpu.VMEM((own_rows * 64, azimuth), F32),
            mail,
            mail,
            mail,
            mail,
            pltpu.VMEM(field, F32),
            pltpu.VMEM(field, F32),
            pltpu.SemaphoreType.DMA((6,)),
            pltpu.SemaphoreType.DMA((2,)),
            pltpu.SemaphoreType.DMA((2,)),
            pltpu.SemaphoreType.DMA((2,)),
            pltpu.SemaphoreType.DMA((2,)),
            pltpu.SemaphoreType.DMA((2,)),
            pltpu.SemaphoreType.DMA((2,)),
            pltpu.SemaphoreType.DMA((4,)),
            pltpu.SemaphoreType.DMA((2,)),
            pltpu.SemaphoreType.DMA((2,)),
            pltpu.SemaphoreType.DMA((5,)),
            pltpu.SemaphoreType.DMA((5,)),
            pltpu.SemaphoreType.REGULAR((2,)),
        ],
        compiler_params=pltpu.CompilerParams(collective_id=0, has_side_effects=True, vmem_limit_bytes=48 << 20),
    )(theta_weights, child, stencil, weights, phase, table, far, vec)
    incoming = incoming.reshape(rows, 2, groups, azimuth).transpose(2, 1, 0, 3)
    child_incoming = child_incoming.reshape(own_rows, 8, 2, groups, columns).transpose(3, 1, 2, 0, 4)
    return incoming, child_incoming.reshape(child_patterns.shape)


def solution(mesh):
    placed = (
        P("clus", None, "samp", None),
        P(),
        P(),
        P(),
        P(None, "samp", None),
        P(None, None, "samp", "clus"),
        P(),
        P(),
    )
    return jax.shard_map(
        functools.partial(per_device, mesh.shape["clus"], mesh.shape["samp"]),
        mesh=mesh,
        in_specs=placed,
        out_specs=(P("clus", None, "samp", None), P("clus", None, "samp", None)),
        check_vma=False,
    )
```

```python
import functools

import jax
import jax.numpy as jnp
from jax import lax
from jax.experimental import pallas as pl
from jax.experimental.pallas import tpu as pltpu
from jax.sharding import PartitionSpec as P

MESH = pl.DeviceIdType.MESH
F32 = jnp.float32
BF16 = jnp.bfloat16


def halves(value):
    high = value.astype(BF16)
    return high, (value - high.astype(F32)).astype(BF16)


def dot(a, b, contract):
    return lax.dot_general(a, b, ((contract[0], contract[1]), ((), ())), preferred_element_type=F32)


def dot3(a_hi, a_lo, b_hi, b_lo, contract):
    return dot(a_hi, b_hi, contract) + (dot(a_hi, b_lo, contract) + dot(a_lo, b_hi, contract))


def swap_groups(value):
    row = lax.broadcasted_iota(jnp.int32, (8, 128), 0)
    group = lax.broadcasted_iota(jnp.int32, (8, 128), 1) // 16
    for bit in (4, 2, 1):
        own, other = (row // bit) % 2, (group // bit) % 2
        rise = pltpu.roll(pltpu.roll(value, 8 - bit, 1), 16 * bit, 2)
        fall = rise if bit == 4 else pltpu.roll(pltpu.roll(value, bit, 1), 128 - 16 * bit, 2)
        value = jnp.where((own == other)[None], value, jnp.where((own < other)[None], rise, fall))
    return value


def window(
    n_clus, n_samp,
    theta, child, stencil_in, weights_in, phase_in, table_in, far_in, vec_in,
    inc_out, child_out,
    stencil, weights, phase, table, far, vec,
    phi_hi, phi_lo, cosine, sine, picks, operators,
    below, above, lhs_hi, lhs_lo, low_hi, low_lo, total_low,
    msg_out, msg_in, back_out, back_in, inc_pair, inc_far,
    in_sem, halo_send, halo_recv, phase_send, phase_recv,
    a2a_send, a2a_recv, own_sem, back_send, back_recv, inc_send, inc_recv, zone,
):
    me = lax.axis_index("clus")
    ring = lax.axis_index("samp")
    up = lax.rem(ring + 1, n_samp)
    down = lax.rem(ring + n_samp - 1, n_samp)
    core = lax.rem(ring, 2)
    pair = ring + 1 - 2 * core
    away = lax.rem(ring + n_samp - 1 + 2 * core, n_samp)
    deep = lax.rem(lax.div(me, 4), 4)
    first_end = jnp.where(ring == 0, 3, 0)
    last_end = jnp.where(ring == n_samp - 1, 1, 0)
    near = me + 4 * (lax.rem(deep + first_end + last_end, 4) - deep)
    columns = child.shape[2]
    azimuth = stencil.shape[1]
    rows = phase.shape[0]
    some = rows // 2
    far_count, clusters = far.shape
    others = pl.ds(0, n_clus - 1)

    loads = [
        pltpu.make_async_copy(source, target, in_sem.at[place])
        for place, (source, target) in enumerate(
            [(stencil_in, stencil), (weights_in, weights), (phase_in, phase), (table_in, table), (far_in, far), (vec_in, vec)]
        )
    ]
    barrier = pltpu.get_barrier_semaphore()
    layers = [(me + 4 * (lax.rem(deep + by, 4) - deep), ring) for by in (1, 3)]
    for peer in [(me, up), (me, down), (near, away)] + layers:
        pl.semaphore_signal(barrier, inc=1, device_id=peer, device_id_type=MESH)
    plane = lax.div(me, 16)
    across = lax.rem(me, 4)

    def greet(step, carry):
        peer = lax.rem(plane + lax.div(step, 4), 4) * 16 + deep * 4 + lax.rem(across + lax.rem(step, 4), 4)
        pl.semaphore_signal(barrier, inc=1, device_id=(peer, ring), device_id_type=MESH)
        return carry

    lax.fori_loop(1, 16, greet, 0)
    for copy in loads:
        copy.start()

    def tell(stage):
        for peer in layers:
            pl.semaphore_signal(zone.at[stage], inc=1, device_id=peer, device_id_type=MESH)

    loads[2].wait()
    pl.semaphore_wait(barrier, 20)
    halos = [
        pltpu.make_async_remote_copy(
            src_ref=child, dst_ref=target, send_sem=halo_send.at[place], recv_sem=halo_recv.at[place],
            device_id=(me, side), device_id_type=MESH,
        )
        for place, (target, side) in enumerate([(below, up), (above, down)])
    ]
    for copy in halos:
        copy.start()
    tilts = [
        pltpu.make_async_remote_copy(
            src_ref=phase, dst_ref=cosine.at[place], send_sem=phase_send.at[place - 1], recv_sem=phase_recv.at[place - 1],
            device_id=peer, device_id_type=MESH,
        )
        for place, peer in ((1, (me, pair)), (2, (near, away)))
    ]
    for copy in tilts:
        copy.start()
    tell(0)

    for row in range(rows):
        cosine[0, row] = jnp.cos(phase[row])
        sine[0, row] = jnp.sin(phase[row])

    pl.semaphore_wait(zone.at[0], 2)
    tell(1)
    loads[0].wait()
    loads[1].wait()

    def build(step, carry):
        first = pl.multiple_of(step * 32, 32)
        places = lax.broadcasted_iota(jnp.int32, (32, azimuth), 0) + first
        total = jnp.zeros((32, azimuth), F32)
        for point in range(stencil.shape[0]):
            total = total + jnp.where(stencil[point : point + 1, :] == places, weights[point : point + 1, :], 0.0)
        high, low = halves(total)
        phi_hi[pl.ds(first, 32), :] = high
        phi_lo[pl.ds(first, 32), :] = low
        return carry

    lax.fori_loop(0, columns // 32, build, 0)
    for copy in loads[3:]:
        copy.wait()

    inner = clusters // n_clus
    spot = lax.broadcasted_iota(jnp.int32, (clusters, clusters), 0)
    lane = lax.broadcasted_iota(jnp.int32, (clusters, clusters), 1)
    named = ((spot // 64) * 16 + spot % 16) * inner + (spot // 16) % inner
    order = jnp.where(named == lane, 1.0, 0.0).astype(BF16)
    partner = far[...]
    partner = (partner % inner) * n_clus + partner // inner
    wanted = dot(order, partner.astype(F32).astype(BF16), ((1,), (1,)))
    kinds = dot(order, vec[...].astype(F32).astype(BF16), ((1,), (1,)))
    put_row = lax.broadcasted_iota(jnp.int32, (16, 128), 0)
    put_lane = lax.broadcasted_iota(jnp.int32, (16, 128), 1)
    tables = []
    for side in range(2):
        total_hi = jnp.zeros((table.shape[0], 128), F32)
        total_lo = jnp.zeros((table.shape[0], 128), F32)
        for row in range(some):
            for part in range(2):
                put = jnp.where(put_row + (64 * part + 16 * row) == put_lane, 1.0, 0.0).astype(BF16)
                high, low = halves(table[:, side * some + row, part, :])
                total_hi = total_hi + dot(high, put, ((1,), (0,)))
                total_lo = total_lo + dot(low, put, ((1,), (0,)))
        tables.append((total_hi.astype(BF16), total_lo.astype(BF16)))
    lane_f = lane.astype(F32)
    kind_f = lax.broadcasted_iota(jnp.int32, (clusters, table.shape[0]), 1).astype(F32)
    for link in range(far_count):
        pick = jnp.where(wanted[:, link : link + 1] == lane_f, 1.0, 0.0).astype(BF16)
        chosen = jnp.where(kinds[:, link : link + 1] == kind_f, 1.0, 0.0).astype(BF16)
        for part in range(4):
            picks[part, link * 64 : (link + 1) * 64, :] = pick[part * 64 : (part + 1) * 64]
        for side, (t_hi, t_lo) in enumerate(tables):
            operator = dot(chosen, t_hi, ((1,), (0,))) + dot(chosen, t_lo, ((1,), (0,)))
            for part in range(4):
                operators[side, part, link * 64 : (link + 1) * 64, :] = operator[part * 64 : (part + 1) * 64]

    for copy in halos:
        copy.wait()

    for row in range(rows):
        total = jnp.zeros((64, columns), F32)
        for step in range(9):
            part = (below, child, above)[step // 3][step % 3]
            total = total + theta[row, step] * part
        high, low = halves(total)
        lhs_hi[row * 64 : (row + 1) * 64, :] = high
        lhs_lo[row * 64 : (row + 1) * 64, :] = low

    pl.semaphore_wait(zone.at[1], 2)
    half_w = lax.broadcasted_iota(jnp.int32, (8, 256), 0) < 4
    turns = (2, 1, 3, 0)

    def mail_plane(turn, outbox, inbox, send_sem, recv_sem):
        block = lax.rem(plane + turn, 4)

        def send(rise, turned):
            target = block * 16 + lax.rem(deep + rise, 4) * 4 + lax.rem(across + turned, 4)
            pltpu.make_async_remote_copy(
                src_ref=outbox.at[target], dst_ref=inbox.at[me], send_sem=send_sem, recv_sem=recv_sem,
                device_id=(target, ring), device_id_type=MESH,
            ).start()

        @pl.loop(0, 4)
        def _(step):
            send(2, step)

        @pl.loop(0, 8)
        def _(step):
            send(1 + 2 * lax.rem(step, 2), lax.div(step, 2))

        @pl.loop(1 if turn == 0 else 0, 4)
        def _(step):
            send(0, step)

    def spans(turn):
        return pl.ds(pl.multiple_of(lax.rem(plane + turn, 4) * 256, 256), 256)

    steps = [(side, turn) for side in range(2) for turn in turns]

    def refine(side, turn):
        lanes = spans(turn)
        span = slice(side * some * 64, (side + 1) * some * 64)
        return dot3(lhs_hi[span, :], lhs_lo[span, :], phi_hi[:, lanes], phi_lo[:, lanes], ((1,), (0,)))

    refined = refine(*steps[0])
    for place, (side, turn) in enumerate(steps):
        block = lax.rem(plane + turn, 4)
        lanes = spans(turn)
        following = refine(*steps[place + 1]) if place + 1 < len(steps) else None
        fields = []
        for row in range(some):
            straight = jnp.zeros((8, 256), F32)
            crossed = jnp.zeros((8, 256), F32)
            for octant in range(8):
                piece = refined[row * 64 + octant * 8 : row * 64 + octant * 8 + 8]
                straight = straight + piece * cosine[0, side * some + row, octant : octant + 1, lanes]
                crossed = crossed + piece * sine[0, side * some + row, octant : octant + 1, lanes]
            crossed = pltpu.roll(crossed, 4, 0)
            field = straight + jnp.where(half_w, -crossed, crossed)
            fields += [field[:, :128], field[:, 128:]]
        packed = swap_groups(jnp.stack(fields, axis=0))
        for row in range(some):
            for part in range(2):
                msg_out[side, pl.ds(block * 16 + part * 8, 8), row, :] = packed[row * 2 + part]
        mail_plane(turn, msg_out.at[side], msg_in.at[side], a2a_send.at[side], a2a_recv.at[side])
        refined = following

    owns = []
    for side in range(2):
        own = pltpu.make_async_copy(msg_out.at[side, me], msg_in.at[side, me], own_sem.at[side])
        own.start()
        owns.append(own)
    group = lax.broadcasted_iota(jnp.int32, (n_clus, 128), 1) // 16 % 4
    small = lax.broadcasted_iota(jnp.int32, (16, 128), 1) // 16 % 4
    real = lax.broadcasted_iota(jnp.int32, (64, 128), 1) < 64
    for side in range(2):
        owns[side].wait()
        pltpu.make_async_copy(msg_out.at[side, others], msg_in.at[side, others], a2a_recv.at[side]).wait()
        arrived = [msg_in[side, :, row, :] for row in range(some)]
        gathered = []
        for seat_in in range(inner):
            total = jnp.zeros((n_clus, 128), F32)
            for row in range(some):
                total = jnp.where(group == row, pltpu.roll(arrived[row], (16 * (row - seat_in)) % 128, 1), total)
            gathered.append(total)
        both = jnp.concatenate(halves(jnp.concatenate(gathered, axis=0)), axis=1)

        def fetch(turn):
            found = dot(picks[lax.rem(plane + turn, 4)], both, ((1,), (0,)))
            return found[:, :128] + found[:, 128:]

        source = fetch(turns[0])
        for place, turn in enumerate(turns):
            block = lax.rem(plane + turn, 4)
            following = fetch(turns[place + 1]) if place < 3 else None
            alike = jnp.zeros((64, 128), F32)
            mixed = jnp.zeros((64, 128), F32)
            for link in range(far_count):
                span = slice(link * 64, (link + 1) * 64)
                piece = source[span]
                operator = operators[side, block, span, :]
                alike = alike + operator * piece
                mixed = mixed + operator * pltpu.roll(piece, 64, 1)
            field = jnp.where(real, alike - pltpu.roll(alike, 64, 1), mixed + pltpu.roll(mixed, 64, 1))
            for row in range(some):
                total = jnp.zeros((16, 128), F32)
                for seat_in in range(inner):
                    piece = field[seat_in * 16 : (seat_in + 1) * 16]
                    total = jnp.where(small == seat_in, pltpu.roll(piece, (16 * (seat_in - row)) % 128, 1), total)
                back_out[side, pl.ds(block * 16, 16), row, :] = total
            mail_plane(turn, back_out.at[side], back_in.at[side], back_send.at[side], back_recv.at[side])
            source = following

    owns = []
    for side in range(2):
        own = pltpu.make_async_copy(back_out.at[side, me], back_in.at[side, me], own_sem.at[2 + side])
        own.start()
        owns.append(own)

    for copy in tilts:
        copy.wait()
    for place in (1, 2):
        for row in range(rows):
            angle = cosine[place, row]
            sine[place, row] = jnp.sin(angle)
            cosine[place, row] = jnp.cos(angle)

    half = lax.broadcasted_iota(jnp.int32, (8, 128), 0) < 4

    def lower(source, place, base, side, blocks):
        last = place == 2 and side == 1
        span_rows = range(side * some, (side + 1) * some)
        scale = [[theta[row, base + step] for step in range(3)] for row in span_rows]
        for block in blocks:
            lanes = slice(block * 128, (block + 1) * 128)
            straight = [source[row, :, lanes] for row in span_rows]
            crossed = []
            for field in straight:
                swapped = pltpu.roll(field, 4, 0)
                crossed.append(jnp.where(half, swapped, -swapped))
            for octant in range(0, 8, 2):
                sums = [[], [], []]
                for one in (octant, octant + 1):
                    totals = [jnp.zeros((8, 128), F32)] * 3
                    for index, row in enumerate(span_rows):
                        piece = (
                            straight[index] * cosine[place, row, one : one + 1, lanes]
                            + crossed[index] * sine[place, row, one : one + 1, lanes]
                        )
                        totals = [total + scale[index][step] * piece for step, total in enumerate(totals)]
                    for step in range(3):
                        sums[step].append(totals[step])
                for step in range(3):
                    span = slice(step * 64 + octant * 8, step * 64 + octant * 8 + 16)
                    value = jnp.concatenate(sums[step], axis=0)
                    if place > 0 or side > 0:
                        value = value + total_low[span, lanes]
                    if not last:
                        total_low[span, lanes] = value
                    else:
                        high, low = halves(value)
                        low_hi[span, lanes] = high
                        low_lo[span, lanes] = low

    blocks = azimuth // 128
    wide = azimuth // 2

    def hand(origin, target, place, side):
        copy = pltpu.make_async_remote_copy(
            src_ref=origin, dst_ref=target, send_sem=inc_send.at[place], recv_sem=inc_recv.at[place],
            device_id=(me, side), device_id_type=MESH,
        )
        copy.start()
        return copy

    passes = []
    for side in range(2):
        owns[side].wait()
        pltpu.make_async_copy(back_out.at[side, others], back_in.at[side, others], back_recv.at[side]).wait()
        for row in range(some):
            field = swap_groups(back_in[side, :, row, :].reshape(n_clus // 8, 8, 128))
            for block in range(blocks):
                inc_out[side * some + row, :, block * 128 : (block + 1) * 128] = field[block]
        span = pl.ds(side * some, some)
        if side == 0:
            passes.append(hand(inc_out.at[span], inc_far.at[span], 0, away))
            passes.append(hand(inc_out.at[span], inc_pair.at[span], 1, pair))
        else:
            for part in range(2):
                cols = pl.ds(part * wide, wide)
                passes.append(hand(inc_out.at[span, :, cols], inc_far.at[span, :, cols], 2 + part, away))
            passes.append(hand(inc_out.at[span], inc_pair.at[span], 4, pair))
        lower(inc_out, 0, 3, side, range(blocks))
    passes[1].wait()
    lower(inc_pair, 1, 6 * core, 0, range(blocks))
    passes[4].wait()
    lower(inc_pair, 1, 6 * core, 1, range(blocks))
    for side in range(2):
        pltpu.make_async_copy(msg_out.at[side, others], msg_in.at[side, others], a2a_send.at[side]).wait()
        pltpu.make_async_copy(back_out.at[side, others], back_in.at[side, others], back_send.at[side]).wait()
    passes[0].wait()
    lower(inc_far, 2, 6 - 6 * core, 0, range(blocks))
    for part in range(2):
        passes[2 + part].wait()
        lower(inc_far, 2, 6 - 6 * core, 1, range(part * blocks // 2, (part + 1) * blocks // 2))
        lanes = slice(part * wide, (part + 1) * wide)
        for cut in range(0, columns, 256):
            span = slice(cut, cut + 256)
            narrow = dot3(low_hi[:, lanes], low_lo[:, lanes], phi_hi[span, lanes], phi_lo[span, lanes], ((1,), (1,)))
            for step in range(3):
                value = narrow[step * 64 : (step + 1) * 64]
                child_out[step, :, span] = value if part == 0 else child_out[step, :, span] + value


def per_device(n_clus, n_samp, child_patterns, theta_weights, phi_stencil, phi_weights, shift_phase, translation_table, far_list, far_vector):
    groups = child_patterns.shape[0] // 8
    own_rows, columns = child_patterns.shape[2:]
    rows = theta_weights.shape[0]
    azimuth = phi_stencil.shape[0]
    clusters, far_count = far_list.shape
    child = child_patterns.reshape(groups, 8, 2, own_rows, columns).transpose(3, 1, 2, 0, 4)
    child = child.reshape(own_rows, groups * 16, columns)
    vmem = pl.BlockSpec(memory_space=pltpu.VMEM)
    smem = pl.BlockSpec(memory_space=pltpu.SMEM)
    hbm = pl.BlockSpec(memory_space=pltpu.HBM)
    block = (own_rows, groups * 16, columns)
    field = (rows, 8, azimuth)
    stencil, weights = phi_stencil.T, phi_weights.T
    phase = shift_phase.transpose(1, 0, 2)
    table = translation_table.transpose(0, 2, 1, 3)
    far, vec = far_list.T, far_vector.T
    mail = pltpu.VMEM((2, n_clus, rows // 2, 128), F32)
    incoming, child_incoming = pl.pallas_call(
        functools.partial(window, n_clus, n_samp),
        out_shape=(jax.ShapeDtypeStruct(field, F32), jax.ShapeDtypeStruct(block, F32)),
        in_specs=[smem, vmem] + [hbm] * 6,
        out_specs=(vmem, vmem),
        scratch_shapes=[
            pltpu.VMEM(stencil.shape, jnp.int32),
            pltpu.VMEM(weights.shape, F32),
            pltpu.VMEM(field, F32),
            pltpu.VMEM(table.shape, F32),
            pltpu.VMEM(far.shape, jnp.int32),
            pltpu.VMEM(vec.shape, jnp.int32),
            pltpu.VMEM((columns, azimuth), BF16),
            pltpu.VMEM((columns, azimuth), BF16),
            pltpu.VMEM((3,) + field, F32),
            pltpu.VMEM((3,) + field, F32),
            pltpu.VMEM((4, far_count * 64, clusters), BF16),
            pltpu.VMEM((2, 4, far_count * 64, 128), F32),
            pltpu.VMEM(block, F32),
            pltpu.VMEM(block, F32),
            pltpu.VMEM((rows * 64, columns), BF16),
            pltpu.VMEM((rows * 64, columns), BF16),
            pltpu.VMEM((own_rows * 64, azimuth), BF16),
            pltpu.VMEM((own_rows * 64, azimuth), BF16),
            pltpu.VMEM((own_rows * 64, azimuth), F32),
            mail,
            mail,
            mail,
            mail,
            pltpu.VMEM(field, F32),
            pltpu.VMEM(field, F32),
            pltpu.SemaphoreType.DMA((6,)),
            pltpu.SemaphoreType.DMA((2,)),
            pltpu.SemaphoreType.DMA((2,)),
            pltpu.SemaphoreType.DMA((2,)),
            pltpu.SemaphoreType.DMA((2,)),
            pltpu.SemaphoreType.DMA((2,)),
            pltpu.SemaphoreType.DMA((2,)),
            pltpu.SemaphoreType.DMA((4,)),
            pltpu.SemaphoreType.DMA((2,)),
            pltpu.SemaphoreType.DMA((2,)),
            pltpu.SemaphoreType.DMA((5,)),
            pltpu.SemaphoreType.DMA((5,)),
            pltpu.SemaphoreType.REGULAR((2,)),
        ],
        compiler_params=pltpu.CompilerParams(collective_id=0, has_side_effects=True, vmem_limit_bytes=48 << 20),
    )(theta_weights, child, *(pltpu.with_memory_space_constraint(x, pltpu.HBM) for x in (stencil, weights, phase, table, far, vec)))
    incoming = incoming.reshape(rows, 2, groups, azimuth).transpose(2, 1, 0, 3)
    child_incoming = child_incoming.reshape(own_rows, 8, 2, groups, columns).transpose(3, 1, 2, 0, 4)
    return incoming, child_incoming.reshape(child_patterns.shape)


def solution(mesh):
    placed = (
        P("clus", None, "samp", None),
        P(),
        P(),
        P(),
        P(None, "samp", None),
        P(None, None, "samp", "clus"),
        P(),
        P(),
    )
    return jax.shard_map(
        functools.partial(per_device, mesh.shape["clus"], mesh.shape["samp"]),
        mesh=mesh,
        in_specs=placed,
        out_specs=(P("clus", None, "samp", None), P("clus", None, "samp", None)),
        check_vma=False,
    )
```
